32 devices in a mesh: seq: 8 (over z, y), head: 4 (over x, core).
Axes of the slice: x: 2, y: 2, z: 4, core: 2. Of those that a mesh axis runs over, the one named last changes fastest.
Arguments:
- queries: bfloat16 [8192, 1024], P('seq', 'head'), may hold values from -0.69921875 to 0.69921875
- key_vectors: bfloat16 [8192, 1024], P('seq', 'head'), may hold values from -0.69921875 to 0.69921875
- values: bfloat16 [8192, 1024], P('seq', 'head'), may hold values from -0.69921875 to 0.69921875
- out_grad: bfloat16 [8192, 1024], P('seq', 'head'), may hold values from -6 to 6
- level_coef: float32 [17, 8192], P(None, 'seq'), may hold values from 0.25 to 4
- saved_states: bfloat16 [8, 6, 8, 128, 128], P('seq', None, 'head'), may hold values from -0.079589844 to 0.079589844
Outputs:
- query_grad: bfloat16 [8192, 1024], P('seq', 'head')
- key_grad: bfloat16 [8192, 1024], P('seq', 'head')
- value_grad: bfloat16 [8192, 1024], P('seq', 'head')
- coef_grad: float32 [17, 8192], P(None, 'seq')
The draws below stay inside these ranges and needn't reach their ends.
All inputs are finite; a program needn't handle non-finite values.
Results may differ from the reference program's by a relative error of at most 0.0053.
Values sent between devices are 32-bit elements; how exact they have to be, the bound alone decides.
No kernel may reach another device: no remote copies, remote signals or barrier semaphores. Data moves between devices by JAX's collectives and lax.ppermute only.
A program may use at most 128 MiB of HBM per device.

```python
import math
import jax
import jax.numpy as jnp
import numpy as np
from jax import lax

HEADS = 8
DK = 128
DV = 128
LOCAL_LEVELS = 11
CROSS_LEVELS = 6
SHARD_TOKENS = 1024
SHARDS = 8
TOKENS = 8192
LEVELS = 17


def steps_of(stream_key, shape, shards, least, high):
    def one(axis_at, shards_of):
        draws = jax.random.uniform(jax.random.fold_in(jax.random.fold_in(stream_key, 6), axis_at), (shards_of,), jnp.float32, least / len(shards), high / len(shards))
        return jnp.repeat(jnp.exp(draws), shape[axis_at] // shards_of).reshape((-1,) + (1,) * (len(shape) - axis_at - 1))

    gain = one(*shards[0])
    for cut in shards[1:]:
        gain = gain * one(*cut)
    return gain


def centred(own_key, shape, width, bound, split=(), kind=jnp.bfloat16):
    result = width * jax.random.normal(own_key, shape, jnp.float32)
    if split:
        result = result * steps_of(own_key, shape, split, -0.22, 0.18)
    return jnp.clip(result, -bound, bound).astype(kind)


def setup_inputs(seed: int = 0) -> dict:
    splits = jax.random.split(jax.random.key(seed), 7)
    queries = centred(splits[0], (TOKENS, HEADS * DK), 0.115, 0.69921875, ((0, 8), (1, 4)))
    key_vectors = centred(splits[1], (TOKENS, HEADS * DK), 0.115, 0.69921875, ((0, 8), (1, 4)))
    values = centred(splits[2], (TOKENS, HEADS * DV), 0.115, 0.69921875, ((0, 8), (1, 4)))
    out_grad = centred(splits[3], (TOKENS, HEADS * DV), 1.0, 6.0, ((0, 8), (1, 4)))
    level_coef = jnp.clip(jnp.exp(math.log(4.0) - 2.7725887 * jax.random.uniform(splits[4], (LEVELS, TOKENS), jnp.float32) ** steps_of(splits[4], (LEVELS, TOKENS), ((1, 8),), -0.2, 0.2)), 0.25, 4.0)
    saved_states = centred(splits[5], (SHARDS, CROSS_LEVELS, HEADS, DK, DV), 0.013, 0.079589844, ((0, 8), (2, 4)))
    return {"queries": queries, "key_vectors": key_vectors, "values": values, "out_grad": out_grad, "level_coef": level_coef, "saved_states": saved_states}


def level_weight(level_idx):
    if level_idx == 0:
        return 1.0
    return 2.0 ** (-(level_idx - 1) / 2.0)


def level_table(row_pos, col_pos, local_levels):
    mixed = jnp.bitwise_xor(row_pos[:, None], col_pos[None, :])
    levels = jnp.zeros(mixed.shape, jnp.int32)
    for bit_pos in range(local_levels - 1):
        levels = levels + (jnp.right_shift(mixed, bit_pos) > 0).astype(jnp.int32)
    return levels


def coef_table(levels, gate_rows, local_levels):
    level_mix = jnp.zeros(levels.shape, jnp.float32)
    for level_idx in range(local_levels):
        level_mix = jnp.where(levels == level_idx, gate_rows[level_idx][:, None] * level_weight(level_idx), level_mix)
    return level_mix


def rounded(array_in):
    return lax.optimization_barrier(array_in.astype(jnp.bfloat16)).astype(jnp.float32)


def one_shard(packed):
    query_heads, key_heads, value_heads, grad_heads, gates_here, states, shard_idx = packed
    query_data = query_heads.astype(jnp.float32)
    key_data = key_heads.astype(jnp.float32)
    value_data = value_heads.astype(jnp.float32)
    grad_data = grad_heads.astype(jnp.float32)
    positions = jnp.arange(SHARD_TOKENS, dtype=jnp.int32)
    levels = level_table(positions, positions, LOCAL_LEVELS)
    causal = positions[None, :] <= positions[:, None]
    level_mix = jnp.where(causal, coef_table(levels, gates_here[:LOCAL_LEVELS], LOCAL_LEVELS), 0.0)
    scores = jnp.einsum("thd,shd->hts", query_data, key_data)
    grad_scores = jnp.einsum("the,she->hts", grad_data, value_data)
    grad_weights = rounded(level_mix[None] * grad_scores)
    weights = rounded(level_mix[None] * scores)
    query_local = jnp.einsum("hts,shd->thd", grad_weights, key_data)
    key_local = jnp.einsum("hts,thd->shd", grad_weights, query_data)
    value_local = jnp.einsum("hts,the->she", weights, grad_data)
    products = jnp.where(causal, jnp.sum(scores * grad_scores, axis=0), 0.0)
    local_grads = jnp.stack([level_weight(level_idx) * jnp.sum(jnp.where(levels == level_idx, products, 0.0), axis=1) for level_idx in range(LOCAL_LEVELS)])
    level_ids = jnp.arange(CROSS_LEVELS, dtype=jnp.int32)
    bit_flags = jnp.bitwise_and(jnp.right_shift(shard_idx, level_ids), 1).astype(jnp.float32)
    cross_gates = gates_here[LOCAL_LEVELS:]
    scaled = rounded(cross_gates[:, :, None, None] * grad_data[None])
    state_grads = jnp.einsum("thd,jthe->jhde", query_data, scaled)
    weight_list = jnp.array([level_weight(LOCAL_LEVELS + level_idx) for level_idx in range(CROSS_LEVELS)], jnp.float32)
    contrib = state_grads * (weight_list * bit_flags)[:, None, None, None]
    projected = jnp.einsum("the,jhde->jthd", grad_data, states.astype(jnp.float32))
    gate_rows = cross_gates * bit_flags[:, None]
    query_grad = query_local + jnp.sum(gate_rows[:, :, None, None] * projected, axis=0)
    cross_grads = bit_flags[:, None] * jnp.sum(projected * query_data[None], axis=(2, 3))
    coef_grad = jnp.concatenate([local_grads, cross_grads], axis=0)
    return query_grad, key_local, value_local, coef_grad, contrib


def reference(queries, key_vectors, values, out_grad, level_coef, saved_states):
    query_heads = queries.reshape(SHARDS, SHARD_TOKENS, HEADS, DK)
    key_heads = key_vectors.reshape(SHARDS, SHARD_TOKENS, HEADS, DK)
    value_heads = values.reshape(SHARDS, SHARD_TOKENS, HEADS, DV)
    grad_heads = out_grad.reshape(SHARDS, SHARD_TOKENS, HEADS, DV)
    gates = level_coef.reshape(LEVELS, SHARDS, SHARD_TOKENS).transpose(1, 0, 2)
    results = lax.map(one_shard, (query_heads, key_heads, value_heads, grad_heads, gates, saved_states, jnp.arange(SHARDS, dtype=jnp.int32)))
    query_grad, key_local, value_local, coef_parts, contrib = results
    grad_state = jnp.zeros((SHARDS, HEADS, DK, DV), jnp.float32)
    shard_ids = np.arange(SHARDS)
    for level_idx in range(CROSS_LEVELS):
        group_size = 2 ** level_idx
        if 2 * group_size <= SHARDS:
            block_sums = contrib[:, level_idx].reshape(SHARDS // group_size, group_size, HEADS, DK, DV).sum(axis=1)
            partner = ((shard_ids >> level_idx) | 1).astype(np.int32)
            receives = ((shard_ids >> level_idx) & 1) == 0
            grad_state = grad_state + jnp.where(jnp.asarray(receives)[:, None, None, None], block_sums[jnp.asarray(partner)], 0.0)
    state_data = rounded(grad_state)
    key_grad = key_local + jnp.einsum("bshe,bhde->bshd", value_heads.astype(jnp.float32), state_data)
    value_grad = value_local + jnp.einsum("bshd,bhde->bshe", key_heads.astype(jnp.float32), state_data)
    return (query_grad.astype(jnp.bfloat16).reshape(TOKENS, HEADS * DK),
            key_grad.astype(jnp.bfloat16).reshape(TOKENS, HEADS * DK),
            value_grad.astype(jnp.bfloat16).reshape(TOKENS, HEADS * DV),
            coef_parts.transpose(1, 0, 2).reshape(LEVELS, TOKENS))
```

```python
import functools

import jax
import jax.numpy as jnp
from jax import lax
from jax.experimental import pallas as pl
from jax.experimental.pallas import tpu as pltpu
from jax.sharding import PartitionSpec as P

LANES = 128


def level_weight(level_idx):
    if level_idx == 0:
        return 1.0
    return 2.0 ** (-(level_idx - 1) / 2.0)


def dot(lhs, rhs):
    return jnp.dot(lhs, rhs, preferred_element_type=jnp.float32)


def state_kernel(local_levels, query_ref, grad_ref, gates_ref, *out_refs):
    grad_t = grad_ref[...].T.astype(jnp.float32)
    query = query_ref[...]
    for level_idx, out_ref in enumerate(out_refs):
        row = local_levels + level_idx
        scaled = (gates_ref[row : row + 1, :] * grad_t).astype(jnp.bfloat16)
        out_ref[0] = dot(scaled, query) * level_weight(row)


def local_kernel(
    local_levels, cross_levels, flags_ref, query_ref, key_ref, value_ref, grad_ref, gates_ref, states_ref,
    query_out, key_out, value_out, coef_out,
    query_t, key_t, grad_t, mix, levels, sums, weights, grad_weights,
):
    head = pl.program_id(0)
    last = pl.num_programs(0) - 1
    tokens = query_ref.shape[0]
    block = LANES
    wide = 2 * block
    base = block.bit_length() - 1

    query_t[...] = query_ref[...].T
    key_t[...] = key_ref[...].T
    grad_t[...] = grad_ref[...].T

    @pl.when(head == 0)
    def _():
        col = lax.broadcasted_iota(jnp.int32, (block, block), 0)
        row = lax.broadcasted_iota(jnp.int32, (block, block), 1)
        mixed = jnp.bitwise_xor(row, col)
        level = jnp.zeros((block, block), jnp.int32)
        for bit_pos in range(base):
            level = level + (jnp.right_shift(mixed, bit_pos) > 0).astype(jnp.int32)
        level = jnp.where(col <= row, level, -1)
        levels[...] = level
        for idx in range(tokens // block):
            tile = jnp.zeros((block, block), jnp.float32)
            for level_idx in range(base + 1):
                gate = gates_ref[level_idx : level_idx + 1, idx * block : (idx + 1) * block]
                tile = jnp.where(level == level_idx, gate * level_weight(level_idx), tile)
            mix[idx] = tile
        sums[...] = jnp.zeros_like(sums)
        coef_out[...] = jnp.zeros_like(coef_out)

    key_acc = [None] * (tokens // block)
    key_out[...] = jnp.zeros_like(key_out)
    value_out[...] = jnp.zeros_like(value_out)
    for t_start in range(0, tokens, wide):
        t_slice = slice(t_start, t_start + wide)
        q_cols = query_t[:, t_slice]
        g_cols = grad_t[:, t_slice]
        level_totals = {}
        for s_start in range(0, t_start, block):
            s_slice = slice(s_start, s_start + block)
            level = ((s_start ^ t_start) // block).bit_length() + base
            gate = gates_ref[level : level + 1, t_slice] * level_weight(level)
            score = dot(key_ref[s_slice, :], q_cols)
            grad_score = dot(value_ref[s_slice, :], g_cols)
            total = jnp.sum(score * grad_score, axis=0, keepdims=True)
            level_totals[level] = level_totals.get(level, 0.0) + total
            weights[s_slice, :] = (gate * score).astype(jnp.bfloat16)
            grad_weights[s_slice, :] = (gate * grad_score).astype(jnp.bfloat16)
        for level, total in level_totals.items():
            coef_out[level : level + 1, t_slice] += total * level_weight(level)
        idx = t_start // block
        level = base + 1
        high = slice(t_start + block, t_start + wide)
        low = slice(t_start, t_start + block)
        score = dot(key_ref[low, :], q_cols)
        grad_score = dot(value_ref[low, :], g_cols)
        product = score * grad_score
        gate = jnp.broadcast_to(gates_ref[level : level + 1, high] * level_weight(level), (block, block))
        tile = jnp.concatenate([mix[idx], gate], axis=1)
        weights[low, :] = (tile * score).astype(jnp.bfloat16)
        grad_weights[low, :] = (tile * grad_score).astype(jnp.bfloat16)
        sums[idx] += product[:, :block]
        coef_out[level : level + 1, high] += (
            jnp.sum(product[:, block:], axis=0, keepdims=True) * level_weight(level)
        )
        score = dot(key_ref[high, :], q_cols[:, block:])
        grad_score = dot(value_ref[high, :], g_cols[:, block:])
        tile = mix[idx + 1]
        zeros = jnp.zeros((block, block), jnp.bfloat16)
        weights[high, :block] = zeros
        grad_weights[high, :block] = zeros
        weights[high, block:] = (tile * score).astype(jnp.bfloat16)
        grad_weights[high, block:] = (tile * grad_score).astype(jnp.bfloat16)
        sums[idx + 1] += score * grad_score

        s_all = slice(0, t_start + wide)
        query_total = dot(key_t[:, s_all], grad_weights[s_all, :])
        for level_idx in range(cross_levels):
            row = local_levels + level_idx
            projected = dot(states_ref[0, level_idx, 0], g_cols)
            flag = flags_ref[level_idx]
            query_total += (gates_ref[row : row + 1, t_slice] * flag) * projected
            coef_out[row : row + 1, t_slice] += flag * jnp.sum(
                q_cols.astype(jnp.float32) * projected, axis=0, keepdims=True
            )
        query_out[t_slice, :] = query_total.astype(jnp.bfloat16).T
        key_out[s_all, :] += dot(grad_weights[s_all, :], query_ref[t_slice, :])
        value_out[s_all, :] += dot(weights[s_all, :], grad_ref[t_slice, :])

    @pl.when(head == last)
    def _():
        level = levels[...]
        for idx in range(tokens // block):
            product = sums[idx]
            for level_idx in range(base + 1):
                picked = jnp.sum(jnp.where(level == level_idx, product, 0.0), axis=0, keepdims=True)
                coef_out[level_idx : level_idx + 1, idx * block : (idx + 1) * block] = (
                    picked * level_weight(level_idx)
                )


def apply_kernel(key_ref, value_ref, key_local, value_local, state_ref, key_out, value_out):
    state = state_ref[0].astype(jnp.bfloat16)
    key_out[...] = (key_local[...] + dot(value_ref[...], state)).astype(jnp.bfloat16)
    value_out[...] = (value_local[...] + dot(key_ref[...], state.T)).astype(jnp.bfloat16)


def shards(queries, key_vectors, values, out_grad, level_coef, saved_states):
    tokens = queries.shape[0]
    cross_levels = saved_states.shape[1]
    head_count = saved_states.shape[2]
    key_width = saved_states.shape[3]
    value_width = saved_states.shape[4]
    level_count = level_coef.shape[0]
    local_levels = level_count - cross_levels
    shard_count = lax.axis_size("seq")
    bit_count = shard_count.bit_length() - 1
    shard_idx = lax.axis_index("seq")

    def head_block(width):
        return pl.BlockSpec((tokens, width), lambda h: (0, h))

    def whole(shape):
        return pl.BlockSpec(shape, lambda h: (0,) * len(shape))

    state_block = pl.BlockSpec((1, value_width, key_width), lambda h: (h, 0, 0))
    state_shape = jax.ShapeDtypeStruct((head_count, value_width, key_width), jnp.float32)
    contrib = pl.pallas_call(
        functools.partial(state_kernel, local_levels),
        grid=(head_count,),
        in_specs=[head_block(key_width), head_block(value_width), whole(level_coef.shape)],
        out_specs=[state_block] * bit_count,
        out_shape=[state_shape] * bit_count,
    )(queries, out_grad, level_coef)

    flags = jnp.bitwise_and(
        jnp.right_shift(shard_idx, jnp.arange(bit_count, dtype=jnp.int32)), 1
    ).astype(jnp.float32)
    block = LANES
    wide = 2 * block
    query_grad, key_local, value_local, coef_local = pl.pallas_call(
        functools.partial(local_kernel, local_levels, bit_count),
        grid=(head_count,),
        in_specs=[
            pl.BlockSpec(memory_space=pltpu.SMEM),
            head_block(key_width), head_block(key_width), head_block(value_width), head_block(value_width),
            whole(level_coef.shape),
            pl.BlockSpec((1, bit_count, 1, key_width, value_width), lambda h: (0, 0, h, 0, 0)),
        ],
        out_specs=[
            head_block(key_width), head_block(key_width), head_block(value_width),
            whole(level_coef.shape),
        ],
        out_shape=[
            jax.ShapeDtypeStruct(queries.shape, jnp.bfloat16),
            jax.ShapeDtypeStruct(queries.shape, jnp.float32),
            jax.ShapeDtypeStruct(values.shape, jnp.float32),
            jax.ShapeDtypeStruct(level_coef.shape, jnp.float32),
        ],
        scratch_shapes=[
            pltpu.VMEM((key_width, tokens), jnp.bfloat16),
            pltpu.VMEM((key_width, tokens), jnp.bfloat16),
            pltpu.VMEM((value_width, tokens), jnp.bfloat16),
            pltpu.VMEM((tokens // block, block, block), jnp.float32),
            pltpu.VMEM((block, block), jnp.int32),
            pltpu.VMEM((tokens // block, block, block), jnp.float32),
            pltpu.VMEM((tokens, wide), jnp.bfloat16),
            pltpu.VMEM((tokens, wide), jnp.bfloat16),
        ],
    )(flags, queries, key_vectors, values, out_grad, level_coef, saved_states)

    def send(value, mask, level_idx, both):
        pairs = [(p, p ^ mask) for p in range(shard_count) if (p >> level_idx) & 1]
        return lax.ppermute(value, "seq", pairs)

    grad_state = None
    for level_idx in reversed(range(bit_count)):
        partial_value = contrib[level_idx]
        for bit_pos in range(level_idx):
            partial_value = partial_value + send(partial_value, 2**bit_pos, level_idx, True)
        received = send(partial_value, 2**level_idx, level_idx, False)
        grad_state = received if grad_state is None else grad_state + received

    coef_grad = coef_local
    head_groups = lax.axis_size("head")
    for bit_pos in range(head_groups.bit_length() - 1):
        pairs = [(p, p ^ 2**bit_pos) for p in range(head_groups)]
        coef_grad = coef_grad + lax.ppermute(coef_grad, "head", pairs)

    key_grad, value_grad = pl.pallas_call(
        apply_kernel,
        grid=(head_count,),
        in_specs=[
            head_block(key_width), head_block(value_width), head_block(key_width), head_block(value_width),
            state_block,
        ],
        out_specs=[head_block(key_width), head_block(value_width)],
        out_shape=[
            jax.ShapeDtypeStruct(queries.shape, jnp.bfloat16),
            jax.ShapeDtypeStruct(values.shape, jnp.bfloat16),
        ],
    )(key_vectors, values, key_local, value_local, grad_state)
    return (query_grad, key_grad, value_grad, coef_grad)


def solution(mesh):
    in_specs = (
        P("seq", "head"),
        P("seq", "head"),
        P("seq", "head"),
        P("seq", "head"),
        P(None, "seq"),
        P("seq", None, "head", None, None),
    )
    out_specs = (P("seq", "head"), P("seq", "head"), P("seq", "head"), P(None, "seq"))
    return jax.shard_map(shards, mesh=mesh, in_specs=in_specs, out_specs=out_specs, check_vma=False)
```

```python
import functools

import jax
import jax.numpy as jnp
from jax import lax
from jax.experimental import pallas as pl
from jax.experimental.pallas import tpu as pltpu
from jax.sharding import PartitionSpec as P

LANES = 128


def level_weight(level_idx):
    if level_idx == 0:
        return 1.0
    return 2.0 ** (-(level_idx - 1) / 2.0)


def dot(lhs, rhs):
    return jnp.dot(lhs, rhs, preferred_element_type=jnp.float32)


def state_gradient(row, flag, query_ref, grad_t, gates_ref):
    scaled = (gates_ref[row : row + 1, :] * grad_t.astype(jnp.float32)).astype(jnp.bfloat16)
    return dot(scaled, query_ref[...]) * (level_weight(row) * flag)


def top_kernel(row, flags_ref, query_ref, grad_ref, gates_ref, out_ref):
    flag = flags_ref[flags_ref.shape[0] - 1]
    out_ref[0] = state_gradient(row, flag, query_ref, grad_ref[...].T, gates_ref)


def local_kernel(
    local_levels, cross_levels, flags_ref, query_ref, key_ref, value_ref, grad_ref, gates_ref, states_ref,
    query_out, key_out, value_out, coef_out, *rest,
):
    state_outs = rest[: cross_levels - 1]
    (
    query_t, key_t, grad_t, mix, levels, sums, weights, grad_weights,
    ) = rest[cross_levels - 1 :]
    head = pl.program_id(0)
    last = pl.num_programs(0) - 1
    tokens = query_ref.shape[0]
    block = LANES
    wide = 2 * block
    base = block.bit_length() - 1

    query_t[...] = query_ref[...].T
    key_t[...] = key_ref[...].T
    grad_t[...] = grad_ref[...].T

    @pl.when(head == 0)
    def _():
        col = lax.broadcasted_iota(jnp.int32, (block, block), 0)
        row = lax.broadcasted_iota(jnp.int32, (block, block), 1)
        mixed = jnp.bitwise_xor(row, col)
        level = jnp.zeros((block, block), jnp.int32)
        for bit_pos in range(base):
            level = level + (jnp.right_shift(mixed, bit_pos) > 0).astype(jnp.int32)
        level = jnp.where(col <= row, level, -1)
        levels[...] = level
        for idx in range(tokens // block):
            tile = jnp.zeros((block, block), jnp.float32)
            for level_idx in range(base + 1):
                gate = gates_ref[level_idx : level_idx + 1, idx * block : (idx + 1) * block]
                tile = jnp.where(level == level_idx, gate * level_weight(level_idx), tile)
            mix[idx] = tile
        sums[...] = jnp.zeros_like(sums)
        coef_out[...] = jnp.zeros_like(coef_out)

    for level_idx, out_ref in enumerate(state_outs):
        out_ref[0] = state_gradient(
            local_levels + level_idx, flags_ref[level_idx], query_ref, grad_t[...], gates_ref
        )
    key_out[...] = jnp.zeros_like(key_out)
    value_out[...] = jnp.zeros_like(value_out)
    for t_start in range(0, tokens, wide):
        t_slice = slice(t_start, t_start + wide)
        q_cols = query_t[:, t_slice]
        g_cols = grad_t[:, t_slice]
        level_totals = {}
        for s_start in range(0, t_start, block):
            s_slice = slice(s_start, s_start + block)
            level = ((s_start ^ t_start) // block).bit_length() + base
            gate = gates_ref[level : level + 1, t_slice] * level_weight(level)
            score = dot(key_ref[s_slice, :], q_cols)
            grad_score = dot(value_ref[s_slice, :], g_cols)
            total = jnp.sum(score * grad_score, axis=0, keepdims=True)
            level_totals[level] = level_totals.get(level, 0.0) + total
            weights[s_slice, :] = (gate * score).astype(jnp.bfloat16)
            grad_weights[s_slice, :] = (gate * grad_score).astype(jnp.bfloat16)
        for level, total in level_totals.items():
            coef_out[level : level + 1, t_slice] += total * level_weight(level)
        idx = t_start // block
        level = base + 1
        high = slice(t_start + block, t_start + wide)
        low = slice(t_start, t_start + block)
        score = dot(key_ref[low, :], q_cols)
        grad_score = dot(value_ref[low, :], g_cols)
        product = score * grad_score
        gate = jnp.broadcast_to(gates_ref[level : level + 1, high] * level_weight(level), (block, block))
        tile = jnp.concatenate([mix[idx], gate], axis=1)
        weights[low, :] = (tile * score).astype(jnp.bfloat16)
        grad_weights[low, :] = (tile * grad_score).astype(jnp.bfloat16)
        sums[idx] += product[:, :block]
        coef_out[level : level + 1, high] += (
            jnp.sum(product[:, block:], axis=0, keepdims=True) * level_weight(level)
        )
        score = dot(key_ref[high, :], q_cols[:, block:])
        grad_score = dot(value_ref[high, :], g_cols[:, block:])
        tile = mix[idx + 1]
        zeros = jnp.zeros((block, block), jnp.bfloat16)
        weights[high, :block] = zeros
        grad_weights[high, :block] = zeros
        weights[high, block:] = (tile * score).astype(jnp.bfloat16)
        grad_weights[high, block:] = (tile * grad_score).astype(jnp.bfloat16)
        sums[idx + 1] += score * grad_score

        s_all = slice(0, t_start + wide)
        query_total = dot(key_t[:, s_all], grad_weights[s_all, :])
        for level_idx in range(cross_levels):
            row = local_levels + level_idx
            projected = dot(states_ref[0, level_idx, 0], g_cols)
            flag = flags_ref[level_idx]
            query_total += (gates_ref[row : row + 1, t_slice] * flag) * projected
            coef_out[row : row + 1, t_slice] += flag * jnp.sum(
                q_cols.astype(jnp.float32) * projected, axis=0, keepdims=True
            )
        query_out[t_slice, :] = query_total.astype(jnp.bfloat16).T
        key_out[s_all, :] += dot(grad_weights[s_all, :], query_ref[t_slice, :])
        value_out[s_all, :] += dot(weights[s_all, :], grad_ref[t_slice, :])

    @pl.when(head == last)
    def _():
        level = levels[...]
        for idx in range(tokens // block):
            product = sums[idx]
            for level_idx in range(base + 1):
                picked = jnp.sum(jnp.where(level == level_idx, product, 0.0), axis=0, keepdims=True)
                coef_out[level_idx : level_idx + 1, idx * block : (idx + 1) * block] = (
                    picked * level_weight(level_idx)
                )


def apply_kernel(key_ref, value_ref, key_local, value_local, state_ref, key_out, value_out):
    state = state_ref[0].astype(jnp.bfloat16)
    key_out[...] = (key_local[...] + dot(value_ref[...], state)).astype(jnp.bfloat16)
    value_out[...] = (value_local[...] + dot(key_ref[...], state.T)).astype(jnp.bfloat16)


def shards(queries, key_vectors, values, out_grad, level_coef, saved_states):
    tokens = queries.shape[0]
    cross_levels = saved_states.shape[1]
    head_count = saved_states.shape[2]
    key_width = saved_states.shape[3]
    value_width = saved_states.shape[4]
    level_count = level_coef.shape[0]
    local_levels = level_count - cross_levels
    shard_count = lax.axis_size("seq")
    bit_count = shard_count.bit_length() - 1
    shard_idx = lax.axis_index("seq")

    def head_block(width):
        return pl.BlockSpec((tokens, width), lambda h: (0, h))

    def whole(shape):
        return pl.BlockSpec(shape, lambda h: (0,) * len(shape))

    state_block = pl.BlockSpec((1, value_width, key_width), lambda h: (h, 0, 0))
    state_shape = jax.ShapeDtypeStruct((head_count, value_width, key_width), jnp.float32)
    flags = jnp.bitwise_and(
        jnp.right_shift(shard_idx, jnp.arange(bit_count, dtype=jnp.int32)), 1
    ).astype(jnp.float32)
    top = pl.pallas_call(
        functools.partial(top_kernel, local_levels + bit_count - 1),
        grid=(head_count,),
        in_specs=[
            pl.BlockSpec(memory_space=pltpu.SMEM),
            head_block(key_width), head_block(value_width), whole(level_coef.shape),
        ],
        out_specs=state_block,
        out_shape=state_shape,
    )(flags, queries, out_grad, level_coef)

    def exchange(value, bit_pos):
        pairs = [(p, p ^ 2**bit_pos) for p in range(shard_count)]
        return lax.ppermute(value, "seq", pairs)

    grad_state = exchange(top, bit_count - 1)
    block = LANES
    wide = 2 * block
    query_grad, key_local, value_local, coef_local, *contrib = pl.pallas_call(
        functools.partial(local_kernel, local_levels, bit_count),
        grid=(head_count,),
        in_specs=[
            pl.BlockSpec(memory_space=pltpu.SMEM),
            head_block(key_width), head_block(key_width), head_block(value_width), head_block(value_width),
            whole(level_coef.shape),
            pl.BlockSpec((1, bit_count, 1, key_width, value_width), lambda h: (0, 0, h, 0, 0)),
        ],
        out_specs=[
            head_block(key_width), head_block(key_width), head_block(value_width),
            whole(level_coef.shape),
        ]
        + [state_block] * (bit_count - 1),
        out_shape=[
            jax.ShapeDtypeStruct(queries.shape, jnp.bfloat16),
            jax.ShapeDtypeStruct(queries.shape, jnp.float32),
            jax.ShapeDtypeStruct(values.shape, jnp.float32),
            jax.ShapeDtypeStruct(level_coef.shape, jnp.float32),
        ]
        + [state_shape] * (bit_count - 1),
        scratch_shapes=[
            pltpu.VMEM((key_width, tokens), jnp.bfloat16),
            pltpu.VMEM((key_width, tokens), jnp.bfloat16),
            pltpu.VMEM((value_width, tokens), jnp.bfloat16),
            pltpu.VMEM((tokens // block, block, block), jnp.float32),
            pltpu.VMEM((block, block), jnp.int32),
            pltpu.VMEM((tokens // block, block, block), jnp.float32),
            pltpu.VMEM((tokens, wide), jnp.bfloat16),
            pltpu.VMEM((tokens, wide), jnp.bfloat16),
        ],
    )(flags, queries, key_vectors, values, out_grad, level_coef, saved_states)

    for level_idx in reversed(range(bit_count - 1)):
        grad_state = grad_state + exchange(grad_state + contrib[level_idx], level_idx)

    coef_grad = coef_local
    head_groups = lax.axis_size("head")
    for bit_pos in range(head_groups.bit_length() - 1):
        pairs = [(p, p ^ 2**bit_pos) for p in range(head_groups)]
        coef_grad = coef_grad + lax.ppermute(coef_grad, "head", pairs)

    key_grad, value_grad = pl.pallas_call(
        apply_kernel,
        grid=(head_count,),
        in_specs=[
            head_block(key_width), head_block(value_width), head_block(key_width), head_block(value_width),
            state_block,
        ],
        out_specs=[head_block(key_width), head_block(value_width)],
        out_shape=[
            jax.ShapeDtypeStruct(queries.shape, jnp.bfloat16),
            jax.ShapeDtypeStruct(values.shape, jnp.bfloat16),
        ],
    )(key_vectors, values, key_local, value_local, grad_state)
    return (query_grad, key_grad, value_grad, coef_grad)


def solution(mesh):
    in_specs = (
        P("seq", "head"),
        P("seq", "head"),
        P("seq", "head"),
        P("seq", "head"),
        P(None, "seq"),
        P("seq", None, "head", None, None),
    )
    out_specs = (P("seq", "head"), P("seq", "head"), P("seq", "head"), P(None, "seq"))
    return jax.shard_map(shards, mesh=mesh, in_specs=in_specs, out_specs=out_specs, check_vma=False)
```

```python
import functools

import jax
import jax.numpy as jnp
from jax import lax
from jax.experimental import pallas as pl
from jax.experimental.pallas import tpu as pltpu
from jax.sharding import PartitionSpec as P

LANES = 128
SUBLANES = 8
MIB = 2**20


def level_weight(level_idx):
    if level_idx == 0:
        return 1.0
    return 2.0 ** (-(level_idx - 1) / 2.0)


def dot(lhs, rhs):
    return jnp.dot(lhs, rhs, preferred_element_type=jnp.float32)


def shard_bit(level_idx):
    return jnp.bitwise_and(jnp.right_shift(lax.axis_index("seq"), level_idx), 1).astype(jnp.float32)


def state_gradients(rows, query, grad_t, gates_ref):
    grad_t = grad_t.astype(jnp.float32)
    scaled = [(gates_ref[row : row + 1, :] * grad_t).astype(jnp.bfloat16) for row in rows]
    return dot(jnp.concatenate(scaled, axis=0), query)


def top_kernel(head_count, level_idx, row, *refs):
    query_hbm, key_hbm, value_hbm, grad_hbm, gates_hbm, states_hbm = refs[:6]
    query, key, value, grad, gates, states, out_ref, sems = refs[6:]
    key_width = query.shape[1] // head_count
    value_width = grad.shape[1] // head_count
    first = [pltpu.make_async_copy(gates_hbm, gates, sems.at[0])]
    for head in range(head_count):
        for source, target, width in ((grad_hbm, grad, value_width), (query_hbm, query, key_width)):
            cols = slice(head * width, (head + 1) * width)
            first.append(pltpu.make_async_copy(source.at[:, cols], target.at[:, cols], sems.at[len(first)]))
    later = []
    for source, target in ((key_hbm, key), (value_hbm, value), (states_hbm, states)):
        later.append(pltpu.make_async_copy(source, target, sems.at[len(first) + len(later)]))
    for copy in first + later:
        copy.start()
    first[0].wait()
    scale = shard_bit(level_idx) * level_weight(row)
    for head in range(head_count):
        first[2 * head + 1].wait()
        grad_t = grad[:, head * value_width : (head + 1) * value_width].T
        first[2 * head + 2].wait()
        keys = slice(head * key_width, (head + 1) * key_width)
        out_ref[head] = state_gradients([row], query[:, keys], grad_t, gates) * scale
    for copy in later:
        copy.wait()


def within_block(block):
    col = lax.broadcasted_iota(jnp.int32, (SUBLANES, block), 0)
    row = jnp.bitwise_and(lax.broadcasted_iota(jnp.int32, (SUBLANES, block), 1), SUBLANES - 1)
    mixed = jnp.bitwise_xor(row, col)
    level = jnp.zeros((SUBLANES, block), jnp.int32)
    for bit_pos in range(SUBLANES.bit_length() - 1):
        level = level + (jnp.right_shift(mixed, bit_pos) > 0).astype(jnp.int32)
    return jnp.where(col <= row, level, -1)


def local_kernel(
    local_levels, cross_levels, head_count,
    query_ref, key_ref, value_ref, grad_ref, gates_ref, states_ref,
    query_out, key_out, value_out, coef_out, *rest,
):
    state_outs = rest[: cross_levels - 1]
    key_t, grad_t, mix, sums, weights, grad_weights = rest[cross_levels - 1 :]
    tokens = query_ref.shape[0]
    key_width = query_ref.shape[1] // head_count
    value_width = value_ref.shape[1] // head_count
    block = LANES
    wide = 2 * block
    base = block.bit_length() - 1
    inner = SUBLANES.bit_length() - 1
    groups = block // SUBLANES

    level_in = within_block(block)
    lane_group = jnp.right_shift(lax.broadcasted_iota(jnp.int32, (SUBLANES, block), 1), inner)
    row_group = jnp.right_shift(lax.broadcasted_iota(jnp.int32, (groups, block), 1), inner)
    col_group = lax.broadcasted_iota(jnp.int32, (groups, block), 0)
    mixed = jnp.bitwise_xor(row_group, col_group)
    level_out = jnp.zeros((groups, block), jnp.int32)
    for bit_pos in range(base - inner):
        level_out = level_out + (jnp.right_shift(mixed, bit_pos) > 0).astype(jnp.int32)
    level_out = jnp.where(col_group < row_group, level_out + inner, -1)

    for idx in range(tokens // block):
        gates = [
            gates_ref[level : level + 1, idx * block : (idx + 1) * block] * level_weight(level)
            for level in range(base + 1)
        ]
        inside = jnp.zeros((SUBLANES, block), jnp.float32)
        for level in range(inner + 1):
            inside = jnp.where(level_in == level, gates[level], inside)
        outside = jnp.zeros((groups, block), jnp.float32)
        for level in range(inner + 1, base + 1):
            outside = jnp.where(level_out == level, gates[level], outside)
        for group in range(groups):
            mix[idx, group * SUBLANES : (group + 1) * SUBLANES, :] = jnp.where(
                lane_group == group, inside, outside[group : group + 1, :]
            )

    def diagonal_sums(product):
        parts = [product[group * SUBLANES : (group + 1) * SUBLANES, :] for group in range(groups)]
        inside = parts[0]
        for group in range(1, groups):
            inside = jnp.where(lane_group == group, parts[group], inside)
        totals = [jnp.where(level_in == level, inside, 0.0) for level in range(inner + 1)]
        for level in range(inner + 1, base + 1):
            picked = parts[0]
            for pair in range(1, len(parts) // 2):
                picked = jnp.where(jnp.right_shift(lane_group, level - inner) == pair, parts[2 * pair], picked)
            right = jnp.bitwise_and(jnp.right_shift(lane_group, level - inner - 1), 1) == 1
            totals.append(jnp.where(right, picked, 0.0))
            parts = [parts[2 * pair] + parts[2 * pair + 1] for pair in range(len(parts) // 2)]
        return [jnp.sum(total, axis=0, keepdims=True) for total in totals]

    for t_start in range(0, tokens, wide):
        t_end = t_start + wide
        t_slice = slice(t_start, t_end)
        idx = t_start // block
        low = slice(t_start, t_start + block)
        high = slice(t_start + block, t_end)
        near = base + 1
        chunks = []
        s_start = 0
        while s_start < t_start:
            level = (s_start ^ t_start).bit_length()
            size = min(1 << (level - 1), t_start - s_start)
            chunks.append((s_start, s_start + size, level))
            s_start += size
        level_sums = {}
        cross_sums = [None] * cross_levels
        for head in range(head_count):
            keys = slice(head * key_width, (head + 1) * key_width)
            vals = slice(head * value_width, (head + 1) * value_width)
            q_cols = query_ref[t_slice, keys].T
            g_cols = grad_ref[t_slice, vals].T
            key_t[head, :, t_slice] = key_ref[t_slice, keys].T
            grad_t[head, :, t_slice] = g_cols
            for s_start, s_end, level in chunks:
                s_slice = slice(s_start, s_end)
                gate = gates_ref[level : level + 1, t_slice] * level_weight(level)
                score = dot(key_ref[s_slice, keys], q_cols)
                grad_score = dot(value_ref[s_slice, vals], g_cols)
                product = jnp.sum((score * grad_score).reshape(-1, SUBLANES, wide), axis=0)
                level_sums[level] = level_sums[level] + product if level in level_sums else product
                weights[s_slice, :] = (gate * score).astype(jnp.bfloat16)
                grad_weights[s_slice, :] = (gate * grad_score).astype(jnp.bfloat16)
            score = dot(key_ref[t_slice, keys], q_cols)
            grad_score = dot(value_ref[t_slice, vals], g_cols)
            product = score * grad_score
            gate = jnp.broadcast_to(gates_ref[near : near + 1, high] * level_weight(near), (block, block))
            tile = jnp.concatenate([mix[idx], gate], axis=1)
            weights[low, :] = (tile * score[:block]).astype(jnp.bfloat16)
            grad_weights[low, :] = (tile * grad_score[:block]).astype(jnp.bfloat16)
            zeros = jnp.zeros((block, block), jnp.bfloat16)
            tile = mix[idx + 1]
            weights[high, :block] = zeros
            grad_weights[high, :block] = zeros
            weights[high, block:] = (tile * score[block:, block:]).astype(jnp.bfloat16)
            grad_weights[high, block:] = (tile * grad_score[block:, block:]).astype(jnp.bfloat16)
            three = [product[:block, :block], product[:block, block:], product[block:, block:]]
            if head > 0:
                three = [part + sums[k] for k, part in enumerate(three)]
            if head < head_count - 1:
                for k, part in enumerate(three):
                    sums[k] = part

            s_all = slice(0, t_end)
            query_total = dot(key_t[head, :, s_all], grad_weights[s_all, :])
            stacked = states_ref[0, :cross_levels, head].reshape(cross_levels * key_width, value_width)
            projected = dot(stacked, g_cols)
            q_wide = q_cols.astype(jnp.float32)
            for level_idx in range(cross_levels):
                row = local_levels + level_idx
                part = projected[level_idx * key_width : (level_idx + 1) * key_width]
                query_total += (gates_ref[row : row + 1, t_slice] * shard_bit(level_idx)) * part
                total = jnp.sum((q_wide * part).reshape(-1, SUBLANES, wide), axis=0)
                cross_sums[level_idx] = total if head == 0 else cross_sums[level_idx] + total
            query_out[t_slice, keys] = query_total.astype(jnp.bfloat16).T
            key_part = dot(grad_weights[s_all, :], query_ref[t_slice, keys])
            value_part = dot(weights[s_all, :], grad_ref[t_slice, vals])
            key_out[t_slice, keys] = key_part[t_start:]
            value_out[t_slice, vals] = value_part[t_start:]
            if t_start:
                key_out[:t_start, keys] += key_part[:t_start]
                value_out[:t_start, vals] += value_part[:t_start]

        for level in range(near + 1, local_levels):
            if level in level_sums:
                total = jnp.sum(level_sums[level], axis=0, keepdims=True) * level_weight(level)
            else:
                total = jnp.zeros((1, wide), jnp.float32)
            coef_out[level : level + 1, t_slice] = total
        coef_out[near : near + 1, low] = jnp.zeros((1, block), jnp.float32)
        coef_out[near : near + 1, high] = jnp.sum(three[1], axis=0, keepdims=True) * level_weight(near)
        for part, where in ((three[0], low), (three[2], high)):
            for level, total in enumerate(diagonal_sums(part)):
                coef_out[level : level + 1, where] = total * level_weight(level)
        for level_idx, total in enumerate(cross_sums):
            row = local_levels + level_idx
            coef_out[row : row + 1, t_slice] = jnp.sum(total, axis=0, keepdims=True) * shard_bit(level_idx)

    level_count = coef_out.shape[0]
    if local_levels + cross_levels < level_count:
        coef_out[local_levels + cross_levels :, :] = jnp.zeros(
            (level_count - local_levels - cross_levels, tokens), jnp.float32
        )
    rows = [local_levels + level_idx for level_idx in range(cross_levels - 1)]
    for head in range(head_count):
        if not rows:
            break
        keys = slice(head * key_width, (head + 1) * key_width)
        stacked = state_gradients(rows, query_ref[:, keys], grad_t[head], gates_ref)
        for level_idx, row in enumerate(rows):
            part = stacked[level_idx * value_width : (level_idx + 1) * value_width]
            state_outs[level_idx][head] = part * (shard_bit(level_idx) * level_weight(row))


def apply_kernel(
    head_count, key_ref, value_ref, key_local, value_local, state_ref, received_ref, coef_ref, coef_received,
    key_out, value_out, coef_out, key_total, value_total, coef_total, sems,
):
    tokens = key_ref.shape[0]
    key_width = key_ref.shape[1] // head_count
    value_width = value_ref.shape[1] // head_count
    wide = 2 * LANES
    coef_total[...] = coef_ref[...] + coef_received[...]
    copies = [pltpu.make_async_copy(coef_total, coef_out, sems.at[0])]
    copies[0].start()
    states = [(state_ref[head] + received_ref[head]).astype(jnp.bfloat16) for head in range(head_count)]
    flipped = [state.T for state in states]
    for start in range(0, tokens, wide):
        part = slice(start, start + wide)
        for head in range(head_count):
            keys = slice(head * key_width, (head + 1) * key_width)
            vals = slice(head * value_width, (head + 1) * value_width)
            key_total[part, keys] = (key_local[part, keys] + dot(value_ref[part, vals], states[head])).astype(
                jnp.bfloat16
            )
            value_total[part, vals] = (value_local[part, vals] + dot(key_ref[part, keys], flipped[head])).astype(
                jnp.bfloat16
            )
        for source, target in ((key_total, key_out), (value_total, value_out)):
            copy = pltpu.make_async_copy(
                source.at[start : start + wide, :], target.at[start : start + wide, :], sems.at[len(copies)]
            )
            copy.start()
            copies.append(copy)
    for copy in copies:
        copy.wait()


def shards(queries, key_vectors, values, out_grad, level_coef, saved_states):
    tokens, key_cols = queries.shape
    value_cols = values.shape[1]
    cross_levels = saved_states.shape[1]
    head_count = saved_states.shape[2]
    key_width = saved_states.shape[3]
    value_width = saved_states.shape[4]
    local_levels = level_coef.shape[0] - cross_levels
    shard_count = lax.axis_size("seq")
    bit_count = shard_count.bit_length() - 1
    block = LANES
    wide = 2 * block
    vmem = pl.BlockSpec(memory_space=pltpu.VMEM)
    hbm = pl.BlockSpec(memory_space=pltpu.HBM)
    state_shape = jax.ShapeDtypeStruct((head_count, value_width, key_width), jnp.float32)

    inputs = (queries, key_vectors, values, out_grad, level_coef, saved_states)
    *inputs, top = pl.pallas_call(
        functools.partial(top_kernel, head_count, bit_count - 1, local_levels + bit_count - 1),
        in_specs=[hbm] * 6,
        out_specs=[vmem] * 7,
        out_shape=[jax.ShapeDtypeStruct(x.shape, x.dtype) for x in inputs] + [state_shape],
        scratch_shapes=[pltpu.SemaphoreType.DMA((2 * head_count + 4,))],
        compiler_params=pltpu.CompilerParams(vmem_limit_bytes=8 * MIB),
    )(*[pltpu.with_memory_space_constraint(x, pltpu.HBM) for x in inputs])

    def exchange(value, axis, bit_pos):
        pairs = [(p, p ^ 2**bit_pos) for p in range(lax.axis_size(axis))]
        return lax.ppermute(value, axis, pairs)

    received = exchange(top, "seq", bit_count - 1)

    flops = 8 * head_count * tokens * tokens * key_width
    query_grad, key_local, value_local, coef_grad, *contrib = pl.pallas_call(
        functools.partial(local_kernel, local_levels, bit_count, head_count),
        in_specs=[vmem] * 6,
        out_specs=[vmem] * (4 + bit_count - 1),
        out_shape=[
            jax.ShapeDtypeStruct(queries.shape, jnp.bfloat16),
            jax.ShapeDtypeStruct(queries.shape, jnp.float32),
            jax.ShapeDtypeStruct(values.shape, jnp.float32),
            jax.ShapeDtypeStruct(level_coef.shape, jnp.float32),
        ]
        + [state_shape] * (bit_count - 1),
        scratch_shapes=[
            pltpu.VMEM((head_count, key_width, tokens), jnp.bfloat16),
            pltpu.VMEM((head_count, value_width, tokens), jnp.bfloat16),
            pltpu.VMEM((tokens // block, block, block), jnp.float32),
            pltpu.VMEM((3, block, block), jnp.float32),
            pltpu.VMEM((tokens, wide), jnp.bfloat16),
            pltpu.VMEM((tokens, wide), jnp.bfloat16),
        ],
        compiler_params=pltpu.CompilerParams(vmem_limit_bytes=24 * MIB),
        cost_estimate=pl.CostEstimate(flops=flops, bytes_accessed=8 * MIB, transcendentals=0),
    )(*inputs)

    grad_state = jnp.zeros(state_shape.shape, jnp.float32)
    for level_idx in reversed(range(bit_count - 1)):
        grad_state = grad_state + received
        received = exchange(grad_state + contrib[level_idx], "seq", level_idx)

    head_bits = lax.axis_size("head").bit_length() - 1
    coef_received = jnp.zeros_like(coef_grad)
    for bit_pos in range(head_bits):
        if bit_pos:
            coef_grad = coef_grad + coef_received
        coef_received = exchange(coef_grad, "head", bit_pos)

    pieces = 2 * (tokens // wide) + 1
    key_grad, value_grad, coef_grad = pl.pallas_call(
        functools.partial(apply_kernel, head_count),
        in_specs=[vmem] * 8,
        out_specs=[hbm] * 3,
        out_shape=[
            jax.ShapeDtypeStruct(queries.shape, jnp.bfloat16),
            jax.ShapeDtypeStruct(values.shape, jnp.bfloat16),
            jax.ShapeDtypeStruct(level_coef.shape, jnp.float32),
        ],
        scratch_shapes=[
            pltpu.VMEM(queries.shape, jnp.bfloat16),
            pltpu.VMEM(values.shape, jnp.bfloat16),
            pltpu.VMEM(level_coef.shape, jnp.float32),
            pltpu.SemaphoreType.DMA((pieces,)),
        ],
        compiler_params=pltpu.CompilerParams(vmem_limit_bytes=12 * MIB),
    )(inputs[1], inputs[2], key_local, value_local, grad_state, received, coef_grad, coef_received)
    return (query_grad, key_grad, value_grad, coef_grad)


def solution(mesh):
    in_specs = (
        P("seq", "head"),
        P("seq", "head"),
        P("seq", "head"),
        P("seq", "head"),
        P(None, "seq"),
        P("seq", None, "head", None, None),
    )
    out_specs = (P("seq", "head"), P("seq", "head"), P("seq", "head"), P(None, "seq"))
    return jax.shard_map(shards, mesh=mesh, in_specs=in_specs, out_specs=out_specs, check_vma=False)
```

```python
import functools

import jax
import jax.numpy as jnp
from jax import lax
from jax.experimental import pallas as pl
from jax.experimental.pallas import tpu as pltpu
from jax.sharding import PartitionSpec as P


LANES = 128
SUBLANES = 8
MIB = 2**20


def level_weight(level_idx):
    if level_idx == 0:
        return 1.0
    return 2.0 ** (-(level_idx - 1) / 2.0)


def dot(lhs, rhs):
    return jnp.dot(lhs, rhs, preferred_element_type=jnp.float32)


def shard_bit(level_idx):
    return jnp.bitwise_and(jnp.right_shift(lax.axis_index("seq"), level_idx), 1).astype(jnp.float32)


def state_gradients(rows, query, grad_t, gates_ref):
    grad_t = grad_t.astype(jnp.float32)
    scaled = [(gates_ref[row : row + 1, :] * grad_t).astype(jnp.bfloat16) for row in rows]
    return dot(jnp.concatenate(scaled, axis=0), query)


def top_kernel(head_count, level_idx, row, *refs):
    query_hbm, key_hbm, value_hbm, grad_hbm, gates_hbm, states_hbm = refs[:6]
    query, key, value, grad, gates, states, *out_refs, sems = refs[6:]
    key_width = query.shape[1] // head_count
    value_width = grad.shape[1] // head_count
    first = [pltpu.make_async_copy(gates_hbm, gates, sems.at[0])]
    for head in range(head_count):
        for source, target, width in ((grad_hbm, grad, value_width), (query_hbm, query, key_width)):
            cols = slice(head * width, (head + 1) * width)
            first.append(pltpu.make_async_copy(source.at[:, cols], target.at[:, cols], sems.at[len(first)]))
    later = []
    for source, target in ((key_hbm, key), (value_hbm, value), (states_hbm, states)):
        later.append(pltpu.make_async_copy(source, target, sems.at[len(first) + len(later)]))
    for copy in first + later:
        copy.start()
    first[0].wait()
    scale = shard_bit(level_idx) * level_weight(row)
    for head in range(head_count):
        first[2 * head + 1].wait()
        grad_t = grad[:, head * value_width : (head + 1) * value_width].T
        first[2 * head + 2].wait()
        keys = slice(head * key_width, (head + 1) * key_width)
        out_refs[head][...] = state_gradients([row], query[:, keys], grad_t, gates) * scale
    for copy in later:
        copy.wait()


def within_block(block):
    col = lax.broadcasted_iota(jnp.int32, (SUBLANES, block), 0)
    row = jnp.bitwise_and(lax.broadcasted_iota(jnp.int32, (SUBLANES, block), 1), SUBLANES - 1)
    mixed = jnp.bitwise_xor(row, col)
    level = jnp.zeros((SUBLANES, block), jnp.int32)
    for bit_pos in range(SUBLANES.bit_length() - 1):
        level = level + (jnp.right_shift(mixed, bit_pos) > 0).astype(jnp.int32)
    return jnp.where(col <= row, level, -1)


def local_kernel(
    local_levels, cross_levels, head_count,
    query_ref, key_ref, value_ref, grad_ref, gates_ref, states_ref,
    query_out, key_out, value_out, coef_out, *rest,
):
    *state_outs, key_t, grad_t, mix, sums, weights, grad_weights = rest
    tokens = query_ref.shape[0]
    key_width = query_ref.shape[1] // head_count
    value_width = value_ref.shape[1] // head_count
    block = LANES
    wide = 2 * block
    base = block.bit_length() - 1
    inner = SUBLANES.bit_length() - 1
    groups = block // SUBLANES

    level_in = within_block(block)
    lane_group = jnp.right_shift(lax.broadcasted_iota(jnp.int32, (SUBLANES, block), 1), inner)
    row_group = jnp.right_shift(lax.broadcasted_iota(jnp.int32, (groups, block), 1), inner)
    col_group = lax.broadcasted_iota(jnp.int32, (groups, block), 0)
    mixed = jnp.bitwise_xor(row_group, col_group)
    level_out = jnp.zeros((groups, block), jnp.int32)
    for bit_pos in range(base - inner):
        level_out = level_out + (jnp.right_shift(mixed, bit_pos) > 0).astype(jnp.int32)
    level_out = jnp.where(col_group < row_group, level_out + inner, -1)

    for idx in range(tokens // block):
        gates = [
            gates_ref[level : level + 1, idx * block : (idx + 1) * block] * level_weight(level)
            for level in range(base + 1)
        ]
        inside = jnp.zeros((SUBLANES, block), jnp.float32)
        for level in range(inner + 1):
            inside = jnp.where(level_in == level, gates[level], inside)
        outside = jnp.zeros((groups, block), jnp.float32)
        for level in range(inner + 1, base + 1):
            outside = jnp.where(level_out == level, gates[level], outside)
        for group in range(groups):
            mix[idx, group * SUBLANES : (group + 1) * SUBLANES, :] = jnp.where(
                lane_group == group, inside, outside[group : group + 1, :]
            )

    def diagonal_sums(product):
        parts = [product[group * SUBLANES : (group + 1) * SUBLANES, :] for group in range(groups)]
        inside = parts[0]
        for group in range(1, groups):
            inside = jnp.where(lane_group == group, parts[group], inside)
        totals = [jnp.where(level_in == level, inside, 0.0) for level in range(inner + 1)]
        for level in range(inner + 1, base + 1):
            picked = parts[0]
            for pair in range(1, len(parts) // 2):
                picked = jnp.where(jnp.right_shift(lane_group, level - inner) == pair, parts[2 * pair], picked)
            right = jnp.bitwise_and(jnp.right_shift(lane_group, level - inner - 1), 1) == 1
            totals.append(jnp.where(right, picked, 0.0))
            parts = [parts[2 * pair] + parts[2 * pair + 1] for pair in range(len(parts) // 2)]
        return [jnp.sum(total, axis=0, keepdims=True) for total in totals]

    for t_start in range(0, tokens, wide):
        t_end = t_start + wide
        t_slice = slice(t_start, t_end)
        idx = t_start // block
        low = slice(t_start, t_start + block)
        high = slice(t_start + block, t_end)
        near = base + 1
        chunks = []
        s_start = 0
        while s_start < t_start:
            level = (s_start ^ t_start).bit_length()
            size = min(1 << (level - 1), t_start - s_start)
            chunks.append((s_start, s_start + size, level))
            s_start += size
        level_sums = {}
        cross_sums = [None] * cross_levels
        for head in range(head_count):
            keys = slice(head * key_width, (head + 1) * key_width)
            vals = slice(head * value_width, (head + 1) * value_width)
            q_cols = query_ref[t_slice, keys].T
            g_cols = grad_ref[t_slice, vals].T
            key_t[head, :, t_slice] = key_ref[t_slice, keys].T
            grad_t[head, :, t_slice] = g_cols
            for s_start, s_end, level in chunks:
                s_slice = slice(s_start, s_end)
                gate = gates_ref[level : level + 1, t_slice] * level_weight(level)
                score = dot(key_ref[s_slice, keys], q_cols)
                grad_score = dot(value_ref[s_slice, vals], g_cols)
                product = jnp.sum((score * grad_score).reshape(-1, SUBLANES, wide), axis=0)
                level_sums[level] = level_sums[level] + product if level in level_sums else product
                weights[s_slice, :] = (gate * score).astype(jnp.bfloat16)
                grad_weights[s_slice, :] = (gate * grad_score).astype(jnp.bfloat16)
            score = dot(key_ref[t_slice, keys], q_cols)
            grad_score = dot(value_ref[t_slice, vals], g_cols)
            product = score * grad_score
            gate = jnp.broadcast_to(gates_ref[near : near + 1, high] * level_weight(near), (block, block))
            tile = jnp.concatenate([mix[idx], gate], axis=1)
            weights[low, :] = (tile * score[:block]).astype(jnp.bfloat16)
            grad_weights[low, :] = (tile * grad_score[:block]).astype(jnp.bfloat16)
            zeros = jnp.zeros((block, block), jnp.bfloat16)
            tile = mix[idx + 1]
            weights[high, :block] = zeros
            grad_weights[high, :block] = zeros
            weights[high, block:] = (tile * score[block:, block:]).astype(jnp.bfloat16)
            grad_weights[high, block:] = (tile * grad_score[block:, block:]).astype(jnp.bfloat16)
            three = [product[:block, :block], product[:block, block:], product[block:, block:]]
            if head > 0:
                three = [part + sums[k] for k, part in enumerate(three)]
            if head < head_count - 1:
                for k, part in enumerate(three):
                    sums[k] = part

            s_all = slice(0, t_end)
            query_total = dot(key_t[head, :, s_all], grad_weights[s_all, :])
            stacked = states_ref[0, :cross_levels, head].reshape(cross_levels * key_width, value_width)
            projected = dot(stacked, g_cols)
            q_wide = q_cols.astype(jnp.float32)
            for level_idx in range(cross_levels):
                row = local_levels + level_idx
                part = projected[level_idx * key_width : (level_idx + 1) * key_width]
                query_total += (gates_ref[row : row + 1, t_slice] * shard_bit(level_idx)) * part
                total = jnp.sum((q_wide * part).reshape(-1, SUBLANES, wide), axis=0)
                cross_sums[level_idx] = total if head == 0 else cross_sums[level_idx] + total
            query_out[t_slice, keys] = query_total.astype(jnp.bfloat16).T
            key_part = dot(grad_weights[s_all, :], query_ref[t_slice, keys])
            value_part = dot(weights[s_all, :], grad_ref[t_slice, vals])
            key_out[t_slice, keys] = key_part[t_start:]
            value_out[t_slice, vals] = value_part[t_start:]
            if t_start:
                key_out[:t_start, keys] += key_part[:t_start]
                value_out[:t_start, vals] += value_part[:t_start]

        for level in range(near + 1, local_levels):
            if level in level_sums:
                total = jnp.sum(level_sums[level], axis=0, keepdims=True) * level_weight(level)
            else:
                total = jnp.zeros((1, wide), jnp.float32)
            coef_out[level : level + 1, t_slice] = total
        coef_out[near : near + 1, low] = jnp.zeros((1, block), jnp.float32)
        coef_out[near : near + 1, high] = jnp.sum(three[1], axis=0, keepdims=True) * level_weight(near)
        for part, where in ((three[0], low), (three[2], high)):
            for level, total in enumerate(diagonal_sums(part)):
                coef_out[level : level + 1, where] = total * level_weight(level)
        for level_idx, total in enumerate(cross_sums):
            row = local_levels + level_idx
            coef_out[row : row + 1, t_slice] = jnp.sum(total, axis=0, keepdims=True) * shard_bit(level_idx)

    level_count = coef_out.shape[0]
    if local_levels + cross_levels < level_count:
        coef_out[local_levels + cross_levels :, :] = jnp.zeros(
            (level_count - local_levels - cross_levels, tokens), jnp.float32
        )
    rows = [local_levels + level_idx for level_idx in range(cross_levels - 1)]
    for head in range(head_count):
        if not rows:
            break
        keys = slice(head * key_width, (head + 1) * key_width)
        stacked = state_gradients(rows, query_ref[:, keys], grad_t[head], gates_ref)
        for level_idx, row in enumerate(rows):
            part = stacked[level_idx * value_width : (level_idx + 1) * value_width]
            state_outs[level_idx * head_count + head][...] = part * (shard_bit(level_idx) * level_weight(row))


def apply_kernel(
    head_count, key_ref, value_ref, key_local, value_local, coef_ref, coef_received, *refs,
):
    state_refs = refs[: 2 * head_count]
    key_out, value_out, coef_out, key_total, value_total, coef_total, sems = refs[2 * head_count :]
    tokens = key_ref.shape[0]
    key_width = key_ref.shape[1] // head_count
    value_width = value_ref.shape[1] // head_count
    wide = 2 * LANES
    coef_total[...] = coef_ref[...] + coef_received[...]
    copies = [pltpu.make_async_copy(coef_total, coef_out, sems.at[0])]
    copies[0].start()
    states = [
        (state_refs[head][...] + state_refs[head_count + head][...]).astype(jnp.bfloat16) for head in range(head_count)
    ]
    flipped = [state.T for state in states]
    for start in range(0, tokens, wide):
        part = slice(start, start + wide)
        for head in range(head_count):
            keys = slice(head * key_width, (head + 1) * key_width)
            vals = slice(head * value_width, (head + 1) * value_width)
            key_total[part, keys] = (key_local[part, keys] + dot(value_ref[part, vals], states[head])).astype(
                jnp.bfloat16
            )
            value_total[part, vals] = (value_local[part, vals] + dot(key_ref[part, keys], flipped[head])).astype(
                jnp.bfloat16
            )
        for source, target in ((key_total, key_out), (value_total, value_out)):
            copy = pltpu.make_async_copy(
                source.at[start : start + wide, :], target.at[start : start + wide, :], sems.at[len(copies)]
            )
            copy.start()
            copies.append(copy)
    for copy in copies:
        copy.wait()


def shards(queries, key_vectors, values, out_grad, level_coef, saved_states):
    tokens, _ = queries.shape
    cross_levels = saved_states.shape[1]
    head_count = saved_states.shape[2]
    key_width = saved_states.shape[3]
    value_width = saved_states.shape[4]
    local_levels = level_coef.shape[0] - cross_levels
    shard_count = lax.axis_size("seq")
    bit_count = shard_count.bit_length() - 1
    block = LANES
    wide = 2 * block
    vmem = pl.BlockSpec(memory_space=pltpu.VMEM)
    hbm = pl.BlockSpec(memory_space=pltpu.HBM)
    state_shape = jax.ShapeDtypeStruct((value_width, key_width), jnp.float32)
    heads = range(head_count)

    inputs = (queries, key_vectors, values, out_grad, level_coef, saved_states)
    count = len(inputs)
    results = pl.pallas_call(
        functools.partial(top_kernel, head_count, bit_count - 1, local_levels + bit_count - 1),
        in_specs=[hbm] * 6,
        out_specs=[vmem] * (count + head_count),
        out_shape=[jax.ShapeDtypeStruct(x.shape, x.dtype) for x in inputs] + [state_shape] * head_count,
        scratch_shapes=[pltpu.SemaphoreType.DMA((2 * head_count + 4,))],
        compiler_params=pltpu.CompilerParams(vmem_limit_bytes=8 * MIB),
    )(*[pltpu.with_memory_space_constraint(x, pltpu.HBM) for x in inputs])
    inputs, tops = results[:count], results[count:]

    def exchange(value, axis, bit_pos):
        pairs = [(p, p ^ 2**bit_pos) for p in range(lax.axis_size(axis))]
        return lax.ppermute(value, axis, pairs)

    received = [exchange(tops[head], "seq", bit_count - 1) for head in heads]

    flops = 8 * head_count * tokens * tokens * key_width
    local_call = pl.pallas_call(
        functools.partial(local_kernel, local_levels, bit_count, head_count),
        in_specs=[vmem] * 6,
        out_specs=[vmem] * (4 + (bit_count - 1) * head_count),
        out_shape=[
            jax.ShapeDtypeStruct(queries.shape, jnp.bfloat16),
            jax.ShapeDtypeStruct(queries.shape, jnp.float32),
            jax.ShapeDtypeStruct(values.shape, jnp.float32),
            jax.ShapeDtypeStruct(level_coef.shape, jnp.float32),
        ]
        + [state_shape] * ((bit_count - 1) * head_count),
        scratch_shapes=[
            pltpu.VMEM((head_count, key_width, tokens), jnp.bfloat16),
            pltpu.VMEM((head_count, value_width, tokens), jnp.bfloat16),
            pltpu.VMEM((tokens // block, block, block), jnp.float32),
            pltpu.VMEM((3, block, block), jnp.float32),
            pltpu.VMEM((tokens, wide), jnp.bfloat16),
            pltpu.VMEM((tokens, wide), jnp.bfloat16),
        ],
        compiler_params=pltpu.CompilerParams(vmem_limit_bytes=24 * MIB),
        cost_estimate=pl.CostEstimate(flops=flops, bytes_accessed=8 * MIB, transcendentals=0),
    )
    query_grad, key_local, value_local, coef_grad, *contrib = local_call(*inputs)

    grad_state = [jnp.zeros(state_shape.shape, jnp.float32) for _ in heads]
    for level_idx in reversed(range(bit_count - 1)):
        for head in heads:
            grad_state[head] = grad_state[head] + received[head]
            own = contrib[level_idx * head_count + head]
            received[head] = exchange(grad_state[head] + own, "seq", level_idx)

    head_bits = lax.axis_size("head").bit_length() - 1
    coef_received = jnp.zeros_like(coef_grad)
    for bit_pos in reversed(range(head_bits)):
        if bit_pos < head_bits - 1:
            coef_grad = coef_grad + coef_received
        coef_received = exchange(coef_grad, "head", bit_pos)

    pieces = 2 * (tokens // wide) + 1
    key_grad, value_grad, coef_grad = pl.pallas_call(
        functools.partial(apply_kernel, head_count),
        in_specs=[vmem] * (6 + 2 * head_count),
        out_specs=[hbm] * 3,
        out_shape=[
            jax.ShapeDtypeStruct(queries.shape, jnp.bfloat16),
            jax.ShapeDtypeStruct(values.shape, jnp.bfloat16),
            jax.ShapeDtypeStruct(level_coef.shape, jnp.float32),
        ],
        scratch_shapes=[
            pltpu.VMEM(queries.shape, jnp.bfloat16),
            pltpu.VMEM(values.shape, jnp.bfloat16),
            pltpu.VMEM(level_coef.shape, jnp.float32),
            pltpu.SemaphoreType.DMA((pieces,)),
        ],
        compiler_params=pltpu.CompilerParams(vmem_limit_bytes=12 * MIB),
    )(inputs[1], inputs[2], key_local, value_local, coef_grad, coef_received, *grad_state, *received)
    return (query_grad, key_grad, value_grad, coef_grad)


def solution(mesh):
    in_specs = (
        P("seq", "head"),
        P("seq", "head"),
        P("seq", "head"),
        P("seq", "head"),
        P(None, "seq"),
        P("seq", None, "head", None, None),
    )
    out_specs = (P("seq", "head"), P("seq", "head"), P("seq", "head"), P(None, "seq"))

    return jax.shard_map(shards, mesh=mesh, in_specs=in_specs, out_specs=out_specs, check_vma=False)
```

```python
import functools

import jax
import jax.numpy as jnp
from jax import lax
from jax.experimental import pallas as pl
from jax.experimental.pallas import tpu as pltpu
from jax.sharding import PartitionSpec as P


LANES = 128
SUBLANES = 8
MIB = 2**20


def level_weight(level_idx):
    if level_idx == 0:
        return 1.0
    return 2.0 ** (-(level_idx - 1) / 2.0)


def dot(lhs, rhs):
    return jnp.dot(lhs, rhs, preferred_element_type=jnp.float32)


def dot_t(lhs, rhs):
    return lax.dot_general(lhs, rhs, (((1,), (1,)), ((), ())), preferred_element_type=jnp.float32)


def chunk_rows(head_count, value_width):
    rows = head_count * value_width
    cut = rows // 2 // 16 * 16
    return ((0, cut), (cut, rows))


def store_rows(refs, chunks, head, state):
    width = state.shape[0]
    for ref, (start, stop) in zip(refs, chunks):
        low, high = max(start, head * width), min(stop, (head + 1) * width)
        if low < high:
            ref[low - start : high - start, :] = state[low - head * width : high - head * width]


def load_rows(refs, chunks, head, width):
    parts = []
    for ref, (start, stop) in zip(refs, chunks):
        low, high = max(start, head * width), min(stop, (head + 1) * width)
        if low < high:
            parts.append(ref[low - start : high - start, :])
    return parts[0] if len(parts) == 1 else jnp.concatenate(parts, axis=0)


def shard_bit(level_idx):
    return jnp.bitwise_and(jnp.right_shift(lax.axis_index("seq"), level_idx), 1).astype(jnp.float32)


def state_gradients(rows, query, grad_t, gates_ref):
    grad_t = grad_t.astype(jnp.float32)
    scaled = [(gates_ref[row : row + 1, :] * grad_t).astype(jnp.bfloat16) for row in rows]
    return dot(jnp.concatenate(scaled, axis=0), query)


def top_kernel(head_count, level_idx, row, *refs):
    query_hbm, key_hbm, value_hbm, grad_hbm, gates_hbm, states_hbm = refs[:6]
    query, key, value, grad, gates, states, grad_t, *out_refs, sems = refs[6:]
    key_width = query.shape[1] // head_count
    value_width = grad.shape[1] // head_count
    chunks = chunk_rows(head_count, value_width)
    first = [pltpu.make_async_copy(gates_hbm, gates, sems.at[0])]
    for head in range(head_count):
        for source, target, width in ((grad_hbm, grad, value_width), (query_hbm, query, key_width)):
            cols = slice(head * width, (head + 1) * width)
            first.append(pltpu.make_async_copy(source.at[:, cols], target.at[:, cols], sems.at[len(first)]))
    later = []
    for source, target in ((key_hbm, key), (value_hbm, value), (states_hbm, states)):
        later.append(pltpu.make_async_copy(source, target, sems.at[len(first) + len(later)]))
    for copy in first + later:
        copy.start()
    first[0].wait()
    scale = shard_bit(level_idx) * level_weight(row)
    for head in range(head_count):
        first[2 * head + 1].wait()
        grad_t[head] = grad[:, head * value_width : (head + 1) * value_width].T
        first[2 * head + 2].wait()
        keys = slice(head * key_width, (head + 1) * key_width)
        store_rows(out_refs, chunks, head, state_gradients([row], query[:, keys], grad_t[head], gates) * scale)
    for copy in later:
        copy.wait()


def within_block(block):
    col = lax.broadcasted_iota(jnp.int32, (SUBLANES, block), 0)
    row = jnp.bitwise_and(lax.broadcasted_iota(jnp.int32, (SUBLANES, block), 1), SUBLANES - 1)
    mixed = jnp.bitwise_xor(row, col)
    level = jnp.zeros((SUBLANES, block), jnp.int32)
    for bit_pos in range(SUBLANES.bit_length() - 1):
        level = level + (jnp.right_shift(mixed, bit_pos) > 0).astype(jnp.int32)
    return jnp.where(col <= row, level, -1)


def local_kernel(
    local_levels, cross_levels, head_count,
    query_ref, key_ref, value_ref, grad_ref, gates_ref, grad_t,
    key_out, value_out, coef_out, grad_weights_out, *rest,
):
    *state_outs, mix, sums, weights = rest
    tokens = query_ref.shape[0]
    key_width = query_ref.shape[1] // head_count
    value_width = value_ref.shape[1] // head_count
    block = LANES
    wide = 2 * block
    base = block.bit_length() - 1
    inner = SUBLANES.bit_length() - 1
    groups = block // SUBLANES

    level_in = within_block(block)
    lane_group = jnp.right_shift(lax.broadcasted_iota(jnp.int32, (SUBLANES, block), 1), inner)
    row_group = jnp.right_shift(lax.broadcasted_iota(jnp.int32, (groups, block), 1), inner)
    col_group = lax.broadcasted_iota(jnp.int32, (groups, block), 0)
    mixed = jnp.bitwise_xor(row_group, col_group)
    level_out = jnp.zeros((groups, block), jnp.int32)
    for bit_pos in range(base - inner):
        level_out = level_out + (jnp.right_shift(mixed, bit_pos) > 0).astype(jnp.int32)
    level_out = jnp.where(col_group < row_group, level_out + inner, -1)

    for idx in range(tokens // block):
        gates = [
            gates_ref[level : level + 1, idx * block : (idx + 1) * block] * level_weight(level)
            for level in range(base + 1)
        ]
        inside = jnp.zeros((SUBLANES, block), jnp.float32)
        for level in range(inner + 1):
            inside = jnp.where(level_in == level, gates[level], inside)
        outside = jnp.zeros((groups, block), jnp.float32)
        for level in range(inner + 1, base + 1):
            outside = jnp.where(level_out == level, gates[level], outside)
        for group in range(groups):
            mix[idx, group * SUBLANES : (group + 1) * SUBLANES, :] = jnp.where(
                lane_group == group, inside, outside[group : group + 1, :]
            )

    def diagonal_sums(product):
        parts = [product[group * SUBLANES : (group + 1) * SUBLANES, :] for group in range(groups)]
        inside = parts[0]
        for group in range(1, groups):
            inside = jnp.where(lane_group == group, parts[group], inside)
        totals = [jnp.where(level_in == level, inside, 0.0) for level in range(inner + 1)]
        for level in range(inner + 1, base + 1):
            picked = parts[0]
            for pair in range(1, len(parts) // 2):
                picked = jnp.where(jnp.right_shift(lane_group, level - inner) == pair, parts[2 * pair], picked)
            right = jnp.bitwise_and(jnp.right_shift(lane_group, level - inner - 1), 1) == 1
            totals.append(jnp.where(right, picked, 0.0))
            parts = [parts[2 * pair] + parts[2 * pair + 1] for pair in range(len(parts) // 2)]
        return [jnp.sum(total, axis=0, keepdims=True) for total in totals]

    for t_start in range(0, tokens, wide):
        t_end = t_start + wide
        t_slice = slice(t_start, t_end)
        idx = t_start // block
        low = slice(t_start, t_start + block)
        high = slice(t_start + block, t_end)
        near = base + 1
        chunks = []
        s_start = 0
        while s_start < t_start:
            level = (s_start ^ t_start).bit_length()
            size = min(1 << (level - 1), t_start - s_start)
            chunks.append((s_start, s_start + size, level))
            s_start += size
        level_sums = {}
        for head in range(head_count):
            keys = slice(head * key_width, (head + 1) * key_width)
            vals = slice(head * value_width, (head + 1) * value_width)
            q_rows = query_ref[t_slice, keys]
            g_rows = grad_ref[t_slice, vals]
            grad_weights = grad_weights_out.at[head, t_start // wide]
            for s_start, s_end, level in chunks:
                s_slice = slice(s_start, s_end)
                gate = gates_ref[level : level + 1, t_slice] * level_weight(level)
                score = dot_t(key_ref[s_slice, keys], q_rows)
                grad_score = dot_t(value_ref[s_slice, vals], g_rows)
                product = jnp.sum((score * grad_score).reshape(-1, SUBLANES, wide), axis=0)
                level_sums[level] = level_sums[level] + product if level in level_sums else product
                weights[s_slice, :] = (gate * score).astype(jnp.bfloat16)
                grad_weights[s_slice, :] = (gate * grad_score).astype(jnp.bfloat16)
            score = dot_t(key_ref[t_slice, keys], q_rows)
            grad_score = dot_t(value_ref[t_slice, vals], g_rows)
            product = score * grad_score
            gate = jnp.broadcast_to(gates_ref[near : near + 1, high] * level_weight(near), (block, block))
            tile = jnp.concatenate([mix[idx], gate], axis=1)
            weights[low, :] = (tile * score[:block]).astype(jnp.bfloat16)
            grad_weights[low, :] = (tile * grad_score[:block]).astype(jnp.bfloat16)
            zeros = jnp.zeros((block, block), jnp.bfloat16)
            tile = mix[idx + 1]
            weights[high, :block] = zeros
            grad_weights[high, :block] = zeros
            weights[high, block:] = (tile * score[block:, block:]).astype(jnp.bfloat16)
            grad_weights[high, block:] = (tile * grad_score[block:, block:]).astype(jnp.bfloat16)
            three = [product[:block, :block], product[:block, block:], product[block:, block:]]
            if head > 0:
                three = [part + sums[k] for k, part in enumerate(three)]
            if head < head_count - 1:
                for k, part in enumerate(three):
                    sums[k] = part

            s_all = slice(0, t_end)
            key_part = dot(grad_weights[s_all, :], q_rows)
            value_part = dot(weights[s_all, :], g_rows)
            key_out[t_slice, keys] = key_part[t_start:]
            value_out[t_slice, vals] = value_part[t_start:]
            if t_start:
                key_out[:t_start, keys] += key_part[:t_start]
                value_out[:t_start, vals] += value_part[:t_start]

        for level in range(near + 1, local_levels):
            if level in level_sums:
                total = jnp.sum(level_sums[level], axis=0, keepdims=True) * level_weight(level)
            else:
                total = jnp.zeros((1, wide), jnp.float32)
            coef_out[level : level + 1, t_slice] = total
        coef_out[near : near + 1, low] = jnp.zeros((1, block), jnp.float32)
        coef_out[near : near + 1, high] = jnp.sum(three[1], axis=0, keepdims=True) * level_weight(near)
        for part, where in ((three[0], low), (three[2], high)):
            for level, total in enumerate(diagonal_sums(part)):
                coef_out[level : level + 1, where] = total * level_weight(level)
    rows = [local_levels + level_idx for level_idx in range(cross_levels - 1)]
    chunks = chunk_rows(head_count, value_width)
    for head in range(head_count):
        if not rows:
            break
        keys = slice(head * key_width, (head + 1) * key_width)
        stacked = state_gradients(rows, query_ref[:, keys], grad_t[head], gates_ref)
        for level_idx, row in enumerate(rows):
            part = stacked[level_idx * value_width : (level_idx + 1) * value_width]
            refs = state_outs[level_idx * len(chunks) : (level_idx + 1) * len(chunks)]
            store_rows(refs, chunks, head, part * (shard_bit(level_idx) * level_weight(row)))


def query_kernel(
    local_levels, cross_levels, head_count,
    query_ref, key_ref, grad_ref, gates_ref, states_ref, grad_weights_ref, coef_ref, query_out, coef_out, key_t,
):
    tokens = query_ref.shape[0]
    key_width = query_ref.shape[1] // head_count
    value_width = grad_ref.shape[1] // head_count
    wide = grad_weights_ref.shape[3]
    coef_out[:local_levels, :] = coef_ref[:local_levels, :]
    level_count = coef_out.shape[0]
    if local_levels + cross_levels < level_count:
        coef_out[local_levels + cross_levels :, :] = jnp.zeros(
            (level_count - local_levels - cross_levels, tokens), jnp.float32
        )
    for t_start in range(0, tokens, wide):
        t_end = t_start + wide
        t_slice = slice(t_start, t_end)
        cross_sums = [None] * cross_levels
        for head in range(head_count):
            keys = slice(head * key_width, (head + 1) * key_width)
            vals = slice(head * value_width, (head + 1) * value_width)
            key_t[head, :, t_slice] = key_ref[t_slice, keys].T
            total = dot(key_t[head, :, :t_end], grad_weights_ref[head, t_start // wide, :t_end, :])
            stacked = states_ref[0, :cross_levels, head].reshape(cross_levels * key_width, value_width)
            projected = dot_t(stacked, grad_ref[t_slice, vals])
            q_wide = query_ref[t_slice, keys].T.astype(jnp.float32)
            for level_idx in range(cross_levels):
                row = local_levels + level_idx
                part = projected[level_idx * key_width : (level_idx + 1) * key_width]
                total += (gates_ref[row : row + 1, t_slice] * shard_bit(level_idx)) * part
                cross = jnp.sum((q_wide * part).reshape(-1, SUBLANES, wide), axis=0)
                cross_sums[level_idx] = cross if head == 0 else cross_sums[level_idx] + cross
            query_out[t_slice, keys] = total.astype(jnp.bfloat16).T
        for level_idx, cross in enumerate(cross_sums):
            row = local_levels + level_idx
            coef_out[row : row + 1, t_slice] = jnp.sum(cross, axis=0, keepdims=True) * shard_bit(level_idx)


def apply_kernel(head_count, heads, chunk_count, last, *refs):
    key_ref, value_ref, key_local, value_local = refs[:4]
    state_refs = refs[4 : 4 + chunk_count]
    received_refs = refs[4 + chunk_count : 4 + 2 * chunk_count]
    tokens = key_ref.shape[0]
    key_width = key_ref.shape[1] // head_count
    value_width = value_ref.shape[1] // head_count
    chunks = chunk_rows(head_count, value_width)[:chunk_count]
    wide = 2 * LANES
    copies = []
    if last:
        coef_ref, coef_received = refs[-11:-9]
        key_out, value_out, coef_out, key_total, value_total, coef_total, sems = refs[-7:]
        coef_total[...] = coef_ref[...] + coef_received[...]
        copies.append(pltpu.make_async_copy(coef_total, coef_out, sems.at[0]))
        copies[0].start()
    else:
        query_ref = refs[4 + 2 * chunk_count]
        query_out, key_out, value_out, key_total, value_total, sems = refs[-6:]
        copies.append(pltpu.make_async_copy(query_ref, query_out, sems.at[0]))
        copies[0].start()
    for place, head in enumerate(heads):
        keys = slice(head * key_width, (head + 1) * key_width)
        vals = slice(head * value_width, (head + 1) * value_width)
        state = load_rows(state_refs, chunks, head, value_width) + load_rows(received_refs, chunks, head, value_width)
        state = state.astype(jnp.bfloat16)
        flipped = state.T
        for start in range(0, tokens, wide):
            part = slice(start, start + wide)
            key_total[place, part, :] = (key_local[part, keys] + dot(value_ref[part, vals], state)).astype(jnp.bfloat16)
            value_total[place, part, :] = (value_local[part, vals] + dot(key_ref[part, keys], flipped)).astype(
                jnp.bfloat16
            )
            for source, target, cols in ((key_total, key_out, keys), (value_total, value_out, vals)):
                copy = pltpu.make_async_copy(source.at[place, part, :], target.at[part, cols], sems.at[len(copies)])
                copy.start()
                copies.append(copy)
    for copy in copies:
        copy.wait()


def shards(queries, key_vectors, values, out_grad, level_coef, saved_states):
    tokens, _ = queries.shape
    cross_levels = saved_states.shape[1]
    head_count = saved_states.shape[2]
    key_width = saved_states.shape[3]
    value_width = saved_states.shape[4]
    local_levels = level_coef.shape[0] - cross_levels
    shard_count = lax.axis_size("seq")
    bit_count = shard_count.bit_length() - 1
    block = LANES
    wide = 2 * block
    vmem = pl.BlockSpec(memory_space=pltpu.VMEM)
    hbm = pl.BlockSpec(memory_space=pltpu.HBM)
    chunks = chunk_rows(head_count, value_width)
    parts = range(len(chunks))
    state_shapes = [jax.ShapeDtypeStruct((stop - start, key_width), jnp.float32) for start, stop in chunks]

    inputs = (queries, key_vectors, values, out_grad, level_coef, saved_states)
    count = len(inputs)
    results = pl.pallas_call(
        functools.partial(top_kernel, head_count, bit_count - 1, local_levels + bit_count - 1),
        in_specs=[hbm] * 6,
        out_specs=[vmem] * (count + 1 + len(chunks)),
        out_shape=[jax.ShapeDtypeStruct(x.shape, x.dtype) for x in inputs]
        + [jax.ShapeDtypeStruct((head_count, value_width, tokens), jnp.bfloat16)]
        + state_shapes,
        scratch_shapes=[pltpu.SemaphoreType.DMA((2 * head_count + 4,))],
        compiler_params=pltpu.CompilerParams(vmem_limit_bytes=8 * MIB),
    )(*[pltpu.with_memory_space_constraint(x, pltpu.HBM) for x in inputs])
    inputs, grad_t, tops = results[:count], results[count], results[count + 1 :]

    def exchange(value, axis, bit_pos):
        pairs = [(p, p ^ 2**bit_pos) for p in range(lax.axis_size(axis))]
        return lax.ppermute(value, axis, pairs)

    received = [exchange(tops[part], "seq", bit_count - 1) for part in parts]

    flops = 8 * head_count * tokens * tokens * key_width
    blocks = tokens // wide
    local_call = pl.pallas_call(
        functools.partial(local_kernel, local_levels, bit_count, head_count),
        in_specs=[vmem] * 6,
        out_specs=[vmem] * (4 + (bit_count - 1) * len(chunks)),
        out_shape=[
            jax.ShapeDtypeStruct(queries.shape, jnp.float32),
            jax.ShapeDtypeStruct(values.shape, jnp.float32),
            jax.ShapeDtypeStruct(level_coef.shape, jnp.float32),
            jax.ShapeDtypeStruct((head_count, blocks, tokens, wide), jnp.bfloat16),
        ]
        + state_shapes * (bit_count - 1),
        scratch_shapes=[
            pltpu.VMEM((tokens // block, block, block), jnp.float32),
            pltpu.VMEM((3, block, block), jnp.float32),
            pltpu.VMEM((tokens, wide), jnp.bfloat16),
        ],
        compiler_params=pltpu.CompilerParams(vmem_limit_bytes=20 * MIB),
        cost_estimate=pl.CostEstimate(flops=flops, bytes_accessed=8 * MIB, transcendentals=0),
    )
    query_call = pl.pallas_call(
        functools.partial(query_kernel, local_levels, bit_count, head_count),
        in_specs=[vmem] * 7,
        out_specs=[vmem] * 2,
        out_shape=[
            jax.ShapeDtypeStruct(queries.shape, jnp.bfloat16),
            jax.ShapeDtypeStruct(level_coef.shape, jnp.float32),
        ],
        scratch_shapes=[pltpu.VMEM((head_count, key_width, tokens), jnp.bfloat16)],
        compiler_params=pltpu.CompilerParams(vmem_limit_bytes=12 * MIB),
        cost_estimate=pl.CostEstimate(flops=flops // 4, bytes_accessed=6 * MIB, transcendentals=0),
    )
    query_in, key_in, value_in, grad_in, gates_in, states_in = inputs
    key_local, value_local, coef_grad, grad_weights, *contrib = local_call(
        query_in, key_in, value_in, grad_in, gates_in, grad_t
    )
    query_grad, coef_grad = query_call(query_in, key_in, grad_in, gates_in, states_in, grad_weights, coef_grad)

    grad_state = [jnp.zeros(shape.shape, jnp.float32) for shape in state_shapes]
    for level_idx in reversed(range(bit_count - 1)):
        for part in parts:
            grad_state[part] = grad_state[part] + received[part]
            own = contrib[level_idx * len(chunks) + part]
            received[part] = exchange(grad_state[part] + own, "seq", level_idx)

    head_bits = lax.axis_size("head").bit_length() - 1
    coef_received = jnp.zeros_like(coef_grad)
    for bit_pos in reversed(range(head_bits)):
        if bit_pos < head_bits - 1:
            coef_grad = coef_grad + coef_received
        coef_received = exchange(coef_grad, "head", bit_pos)

    shapes = [
        jax.ShapeDtypeStruct(queries.shape, jnp.bfloat16),
        jax.ShapeDtypeStruct(values.shape, jnp.bfloat16),
    ]
    coef_shape = jax.ShapeDtypeStruct(level_coef.shape, jnp.float32)
    early = [head for head in range(head_count) if (head + 1) * value_width <= chunks[0][1]]
    late = [head for head in range(head_count) if head not in early]
    common = (inputs[1], inputs[2], key_local, value_local)

    def apply_call(which, chunk_count, last):
        pieces = 2 * len(which) * (tokens // wide) + 1
        in_count = 4 + 2 * chunk_count + 1 + last
        return pl.pallas_call(
            functools.partial(apply_kernel, head_count, which, chunk_count, last),
            in_specs=[vmem] * in_count + [hbm] * (2 * last),
            out_specs=[hbm] * 3,
            out_shape=shapes + [coef_shape] if last else shapes[:1] + shapes,
            input_output_aliases={in_count: 0, in_count + 1: 1} if last else {},
            scratch_shapes=[
                pltpu.VMEM((len(which), tokens, key_width), jnp.bfloat16),
                pltpu.VMEM((len(which), tokens, value_width), jnp.bfloat16),
            ]
            + [pltpu.VMEM(level_coef.shape, jnp.float32)] * last
            + [pltpu.SemaphoreType.DMA((pieces,))],
            compiler_params=pltpu.CompilerParams(vmem_limit_bytes=12 * MIB),
        )

    query_grad, *outs = apply_call(early, 1, False)(*common, grad_state[0], received[0], query_grad)
    outs = [pltpu.with_memory_space_constraint(x, pltpu.HBM) for x in outs]
    key_grad, value_grad, coef_grad = apply_call(late, 2, True)(
        *common, *grad_state, *received, coef_grad, coef_received, *outs
    )
    return (query_grad, key_grad, value_grad, coef_grad)


def solution(mesh):
    in_specs = (
        P("seq", "head"),
        P("seq", "head"),
        P("seq", "head"),
        P("seq", "head"),
        P(None, "seq"),
        P("seq", None, "head", None, None),
    )
    out_specs = (P("seq", "head"), P("seq", "head"), P("seq", "head"), P(None, "seq"))

    return jax.shard_map(shards, mesh=mesh, in_specs=in_specs, out_specs=out_specs, check_vma=False)
```

```python
import functools

import jax
import jax.numpy as jnp
from jax import lax
from jax.experimental import pallas as pl
from jax.experimental.pallas import tpu as pltpu
from jax.sharding import PartitionSpec as P


LANES = 128
TOP_PIECES = 2
SUBLANES = 8
MIB = 2**20


def level_weight(level_idx):
    if level_idx == 0:
        return 1.0
    return 2.0 ** (-(level_idx - 1) / 2.0)


def dot(lhs, rhs):
    return jnp.dot(lhs, rhs, preferred_element_type=jnp.float32)


def dot_t(lhs, rhs):
    return lax.dot_general(lhs, rhs, (((1,), (1,)), ((), ())), preferred_element_type=jnp.float32)


def chunk_rows(head_count, value_width):
    rows = head_count * value_width
    cut = rows // 2 // 16 * 16
    return ((0, cut), (cut, rows))


def store_rows(refs, chunks, head, state):
    width = state.shape[0]
    for ref, (start, stop) in zip(refs, chunks):
        low, high = max(start, head * width), min(stop, (head + 1) * width)
        if low < high:
            ref[low - start : high - start, :] = state[low - head * width : high - head * width]


def load_rows(refs, chunks, head, width):
    parts = []
    for ref, (start, stop) in zip(refs, chunks):
        low, high = max(start, head * width), min(stop, (head + 1) * width)
        if low < high:
            parts.append(ref[low - start : high - start, :])
    return parts[0] if len(parts) == 1 else jnp.concatenate(parts, axis=0)


def shard_bit(level_idx):
    return jnp.bitwise_and(jnp.right_shift(lax.axis_index("seq"), level_idx), 1).astype(jnp.float32)


def state_gradients(rows, query, grad_t, gates_ref):
    grad_t = grad_t.astype(jnp.float32)
    scaled = [(gates_ref[row : row + 1, :] * grad_t).astype(jnp.bfloat16) for row in rows]
    return dot(jnp.concatenate(scaled, axis=0), query)


def top_kernel(head_count, level_idx, row, *refs):
    query_hbm, key_hbm, value_hbm, grad_hbm, gates_hbm, states_hbm = refs[:6]
    query, key, value, grad, gates, states, grad_t, *out_refs, sems = refs[6:]
    key_width = query.shape[1] // head_count
    value_width = grad.shape[1] // head_count
    chunks = chunk_rows(head_count, value_width)
    size = query.shape[0] // TOP_PIECES
    spans = [slice(part * size, (part + 1) * size) for part in range(TOP_PIECES)]
    levels = slice(0, level_idx + 1)
    pairs = [(gates_hbm, gates)]
    for span in spans:
        pairs += [(grad_hbm.at[span, :], grad.at[span, :]), (query_hbm.at[span, :], query.at[span, :])]
    pairs += [(key_hbm, key), (value_hbm, value), (states_hbm.at[:, levels], states.at[:, levels])]
    copies = [pltpu.make_async_copy(source, target, sems.at[k]) for k, (source, target) in enumerate(pairs)]
    for copy in copies:
        copy.start()
    copies[0].wait()
    totals = [0.0] * head_count
    for part, span in enumerate(spans):
        copies[1 + 2 * part].wait()
        copies[2 + 2 * part].wait()
        for head in range(head_count):
            keys = slice(head * key_width, (head + 1) * key_width)
            flipped = grad[span, head * value_width : (head + 1) * value_width].T
            grad_t[head, :, span] = flipped
            totals[head] += state_gradients([row], query[span, keys], flipped, gates.at[:, span])
    scale = shard_bit(level_idx) * level_weight(row)
    for head, total in enumerate(totals):
        store_rows(out_refs, chunks, head, total * scale)
    for copy in copies[1 + 2 * len(spans) :]:
        copy.wait()


def within_block(block):
    col = lax.broadcasted_iota(jnp.int32, (SUBLANES, block), 0)
    row = jnp.bitwise_and(lax.broadcasted_iota(jnp.int32, (SUBLANES, block), 1), SUBLANES - 1)
    mixed = jnp.bitwise_xor(row, col)
    level = jnp.zeros((SUBLANES, block), jnp.int32)
    for bit_pos in range(SUBLANES.bit_length() - 1):
        level = level + (jnp.right_shift(mixed, bit_pos) > 0).astype(jnp.int32)
    return jnp.where(col <= row, level, -1)


def local_kernel(
    local_levels, cross_levels, head_count,
    query_ref, key_ref, value_ref, grad_ref, gates_ref, grad_t,
    key_out, value_out, coef_out, grad_weights_out, *rest,
):
    *state_outs, mix, sums, weights = rest
    tokens = query_ref.shape[0]
    key_width = query_ref.shape[1] // head_count
    value_width = value_ref.shape[1] // head_count
    block = LANES
    wide = 2 * block
    base = block.bit_length() - 1
    inner = SUBLANES.bit_length() - 1
    groups = block // SUBLANES

    level_in = within_block(block)
    lane_group = jnp.right_shift(lax.broadcasted_iota(jnp.int32, (SUBLANES, block), 1), inner)
    row_group = jnp.right_shift(lax.broadcasted_iota(jnp.int32, (groups, block), 1), inner)
    col_group = lax.broadcasted_iota(jnp.int32, (groups, block), 0)
    mixed = jnp.bitwise_xor(row_group, col_group)
    level_out = jnp.zeros((groups, block), jnp.int32)
    for bit_pos in range(base - inner):
        level_out = level_out + (jnp.right_shift(mixed, bit_pos) > 0).astype(jnp.int32)
    level_out = jnp.where(col_group < row_group, level_out + inner, -1)

    for idx in range(tokens // block):
        gates = [
            gates_ref[level : level + 1, idx * block : (idx + 1) * block] * level_weight(level)
            for level in range(base + 1)
        ]
        inside = jnp.zeros((SUBLANES, block), jnp.float32)
        for level in range(inner + 1):
            inside = jnp.where(level_in == level, gates[level], inside)
        outside = jnp.zeros((groups, block), jnp.float32)
        for level in range(inner + 1, base + 1):
            outside = jnp.where(level_out == level, gates[level], outside)
        for group in range(groups):
            mix[idx, group * SUBLANES : (group + 1) * SUBLANES, :] = jnp.where(
                lane_group == group, inside, outside[group : group + 1, :]
            )

    def diagonal_sums(product):
        parts = [product[group * SUBLANES : (group + 1) * SUBLANES, :] for group in range(groups)]
        inside = parts[0]
        for group in range(1, groups):
            inside = jnp.where(lane_group == group, parts[group], inside)
        totals = [jnp.where(level_in == level, inside, 0.0) for level in range(inner + 1)]
        for level in range(inner + 1, base + 1):
            picked = parts[0]
            for pair in range(1, len(parts) // 2):
                picked = jnp.where(jnp.right_shift(lane_group, level - inner) == pair, parts[2 * pair], picked)
            right = jnp.bitwise_and(jnp.right_shift(lane_group, level - inner - 1), 1) == 1
            totals.append(jnp.where(right, picked, 0.0))
            parts = [parts[2 * pair] + parts[2 * pair + 1] for pair in range(len(parts) // 2)]
        return [jnp.sum(total, axis=0, keepdims=True) for total in totals]

    for t_start in range(0, tokens, wide):
        t_end = t_start + wide
        t_slice = slice(t_start, t_end)
        idx = t_start // block
        low = slice(t_start, t_start + block)
        high = slice(t_start + block, t_end)
        near = base + 1
        chunks = []
        s_start = 0
        while s_start < t_start:
            level = (s_start ^ t_start).bit_length()
            size = min(1 << (level - 1), t_start - s_start)
            chunks.append((s_start, s_start + size, level))
            s_start += size
        level_sums = {}
        for head in range(head_count):
            keys = slice(head * key_width, (head + 1) * key_width)
            vals = slice(head * value_width, (head + 1) * value_width)
            q_rows = query_ref[t_slice, keys]
            g_rows = grad_ref[t_slice, vals]
            grad_weights = grad_weights_out.at[head, t_start // wide]
            for s_start, s_end, level in chunks:
                s_slice = slice(s_start, s_end)
                gate = gates_ref[level : level + 1, t_slice] * level_weight(level)
                score = dot_t(key_ref[s_slice, keys], q_rows)
                grad_score = dot_t(value_ref[s_slice, vals], g_rows)
                product = jnp.sum((score * grad_score).reshape(-1, SUBLANES, wide), axis=0)
                level_sums[level] = level_sums[level] + product if level in level_sums else product
                weights[s_slice, :] = (gate * score).astype(jnp.bfloat16)
                grad_weights[s_slice, :] = (gate * grad_score).astype(jnp.bfloat16)
            score = dot_t(key_ref[t_slice, keys], q_rows)
            grad_score = dot_t(value_ref[t_slice, vals], g_rows)
            product = score * grad_score
            gate = jnp.broadcast_to(gates_ref[near : near + 1, high] * level_weight(near), (block, block))
            tile = jnp.concatenate([mix[idx], gate], axis=1)
            weights[low, :] = (tile * score[:block]).astype(jnp.bfloat16)
            grad_weights[low, :] = (tile * grad_score[:block]).astype(jnp.bfloat16)
            zeros = jnp.zeros((block, block), jnp.bfloat16)
            tile = mix[idx + 1]
            weights[high, :block] = zeros
            grad_weights[high, :block] = zeros
            weights[high, block:] = (tile * score[block:, block:]).astype(jnp.bfloat16)
            grad_weights[high, block:] = (tile * grad_score[block:, block:]).astype(jnp.bfloat16)
            three = [product[:block, :block], product[:block, block:], product[block:, block:]]
            if head > 0:
                three = [part + sums[k] for k, part in enumerate(three)]
            if head < head_count - 1:
                for k, part in enumerate(three):
                    sums[k] = part

            s_all = slice(0, t_end)
            key_part = dot(grad_weights[s_all, :], q_rows)
            value_part = dot(weights[s_all, :], g_rows)
            key_out[t_slice, keys] = key_part[t_start:]
            value_out[t_slice, vals] = value_part[t_start:]
            if t_start:
                key_out[:t_start, keys] += key_part[:t_start]
                value_out[:t_start, vals] += value_part[:t_start]

        for level in range(near + 1, local_levels):
            if level in level_sums:
                total = jnp.sum(level_sums[level], axis=0, keepdims=True) * level_weight(level)
            else:
                total = jnp.zeros((1, wide), jnp.float32)
            coef_out[level : level + 1, t_slice] = total
        coef_out[near : near + 1, low] = jnp.zeros((1, block), jnp.float32)
        coef_out[near : near + 1, high] = jnp.sum(three[1], axis=0, keepdims=True) * level_weight(near)
        for part, where in ((three[0], low), (three[2], high)):
            for level, total in enumerate(diagonal_sums(part)):
                coef_out[level : level + 1, where] = total * level_weight(level)
    rows = [local_levels + level_idx for level_idx in range(cross_levels - 1)]
    chunks = chunk_rows(head_count, value_width)
    for head in range(head_count):
        if not rows:
            break
        keys = slice(head * key_width, (head + 1) * key_width)
        stacked = state_gradients(rows, query_ref[:, keys], grad_t[head], gates_ref)
        for level_idx, row in enumerate(rows):
            part = stacked[level_idx * value_width : (level_idx + 1) * value_width]
            refs = state_outs[level_idx * len(chunks) : (level_idx + 1) * len(chunks)]
            store_rows(refs, chunks, head, part * (shard_bit(level_idx) * level_weight(row)))


def query_kernel(
    local_levels, cross_levels, head_count,
    query_ref, key_ref, grad_ref, gates_ref, states_ref, grad_weights_ref, coef_ref, query_out, coef_out, key_t,
):
    tokens = query_ref.shape[0]
    key_width = query_ref.shape[1] // head_count
    value_width = grad_ref.shape[1] // head_count
    wide = grad_weights_ref.shape[3]
    coef_out[:local_levels, :] = coef_ref[:local_levels, :]
    level_count = coef_out.shape[0]
    if local_levels + cross_levels < level_count:
        coef_out[local_levels + cross_levels :, :] = jnp.zeros(
            (level_count - local_levels - cross_levels, tokens), jnp.float32
        )
    for t_start in range(0, tokens, wide):
        t_end = t_start + wide
        t_slice = slice(t_start, t_end)
        cross_sums = [None] * cross_levels
        for head in range(head_count):
            keys = slice(head * key_width, (head + 1) * key_width)
            vals = slice(head * value_width, (head + 1) * value_width)
            key_t[head, :, t_slice] = key_ref[t_slice, keys].T
            total = dot(key_t[head, :, :t_end], grad_weights_ref[head, t_start // wide, :t_end, :])
            stacked = states_ref[0, :cross_levels, head].reshape(cross_levels * key_width, value_width)
            projected = dot_t(stacked, grad_ref[t_slice, vals])
            q_wide = query_ref[t_slice, keys].T.astype(jnp.float32)
            for level_idx in range(cross_levels):
                row = local_levels + level_idx
                part = projected[level_idx * key_width : (level_idx + 1) * key_width]
                total += (gates_ref[row : row + 1, t_slice] * shard_bit(level_idx)) * part
                cross = jnp.sum((q_wide * part).reshape(-1, SUBLANES, wide), axis=0)
                cross_sums[level_idx] = cross if head == 0 else cross_sums[level_idx] + cross
            query_out[t_slice, keys] = total.astype(jnp.bfloat16).T
        for level_idx, cross in enumerate(cross_sums):
            row = local_levels + level_idx
            coef_out[row : row + 1, t_slice] = jnp.sum(cross, axis=0, keepdims=True) * shard_bit(level_idx)


def apply_kernel(head_count, heads, chunk_count, last, *refs):
    key_ref, value_ref, key_local, value_local = refs[:4]
    state_refs = refs[4 : 4 + chunk_count]
    received_refs = refs[4 + chunk_count : 4 + 2 * chunk_count]
    tokens = key_ref.shape[0]
    key_width = key_ref.shape[1] // head_count
    value_width = value_ref.shape[1] // head_count
    chunks = chunk_rows(head_count, value_width)[:chunk_count]
    wide = 2 * LANES
    copies = []
    if last:
        coef_ref, coef_received = refs[-11:-9]
        key_out, value_out, coef_out, key_total, value_total, coef_total, sems = refs[-7:]
        coef_total[...] = coef_ref[...] + coef_received[...]
        copies.append(pltpu.make_async_copy(coef_total, coef_out, sems.at[0]))
        copies[0].start()
    else:
        query_ref = refs[4 + 2 * chunk_count]
        query_out, key_out, value_out, key_total, value_total, sems = refs[-6:]
        copies.append(pltpu.make_async_copy(query_ref, query_out, sems.at[0]))
        copies[0].start()
    for place, head in enumerate(heads):
        keys = slice(head * key_width, (head + 1) * key_width)
        vals = slice(head * value_width, (head + 1) * value_width)
        state = load_rows(state_refs, chunks, head, value_width) + load_rows(received_refs, chunks, head, value_width)
        state = state.astype(jnp.bfloat16)
        for start in range(0, tokens, wide):
            part = slice(start, start + wide)
            key_total[place, part, :] = (key_local[part, keys] + dot(value_ref[part, vals], state)).astype(jnp.bfloat16)
            value_total[place, part, :] = (value_local[part, vals] + dot_t(key_ref[part, keys], state)).astype(
                jnp.bfloat16
            )
            for source, target, cols in ((key_total, key_out, keys), (value_total, value_out, vals)):
                copy = pltpu.make_async_copy(source.at[place, part, :], target.at[part, cols], sems.at[len(copies)])
                copy.start()
                copies.append(copy)
    for copy in copies:
        copy.wait()


def shards(queries, key_vectors, values, out_grad, level_coef, saved_states):
    tokens, _ = queries.shape
    cross_levels = saved_states.shape[1]
    head_count = saved_states.shape[2]
    key_width = saved_states.shape[3]
    value_width = saved_states.shape[4]
    local_levels = level_coef.shape[0] - cross_levels
    shard_count = lax.axis_size("seq")
    bit_count = shard_count.bit_length() - 1
    block = LANES
    wide = 2 * block
    vmem = pl.BlockSpec(memory_space=pltpu.VMEM)
    hbm = pl.BlockSpec(memory_space=pltpu.HBM)
    chunks = chunk_rows(head_count, value_width)
    parts = range(len(chunks))
    state_shapes = [jax.ShapeDtypeStruct((stop - start, key_width), jnp.float32) for start, stop in chunks]

    inputs = (queries, key_vectors, values, out_grad, level_coef, saved_states)
    count = len(inputs)
    results = pl.pallas_call(
        functools.partial(top_kernel, head_count, bit_count - 1, local_levels + bit_count - 1),
        in_specs=[hbm] * 6,
        out_specs=[vmem] * (count + 1 + len(chunks)),
        out_shape=[jax.ShapeDtypeStruct(x.shape, x.dtype) for x in inputs]
        + [jax.ShapeDtypeStruct((head_count, value_width, tokens), jnp.bfloat16)]
        + state_shapes,
        scratch_shapes=[pltpu.SemaphoreType.DMA((2 * TOP_PIECES + 4,))],
        compiler_params=pltpu.CompilerParams(vmem_limit_bytes=8 * MIB),
    )(*[pltpu.with_memory_space_constraint(x, pltpu.HBM) for x in inputs])
    inputs, grad_t, tops = results[:count], results[count], results[count + 1 :]

    def exchange(value, axis, bit_pos):
        pairs = [(p, p ^ 2**bit_pos) for p in range(lax.axis_size(axis))]
        return lax.ppermute(value, axis, pairs)

    received = [exchange(tops[part], "seq", bit_count - 1) for part in parts]

    flops = 8 * head_count * tokens * tokens * key_width
    blocks = tokens // wide
    local_call = pl.pallas_call(
        functools.partial(local_kernel, local_levels, bit_count, head_count),
        in_specs=[vmem] * 6,
        out_specs=[vmem] * (4 + (bit_count - 1) * len(chunks)),
        out_shape=[
            jax.ShapeDtypeStruct(queries.shape, jnp.float32),
            jax.ShapeDtypeStruct(values.shape, jnp.float32),
            jax.ShapeDtypeStruct(level_coef.shape, jnp.float32),
            jax.ShapeDtypeStruct((head_count, blocks, tokens, wide), jnp.bfloat16),
        ]
        + state_shapes * (bit_count - 1),
        scratch_shapes=[
            pltpu.VMEM((tokens // block, block, block), jnp.float32),
            pltpu.VMEM((3, block, block), jnp.float32),
            pltpu.VMEM((tokens, wide), jnp.bfloat16),
        ],
        compiler_params=pltpu.CompilerParams(vmem_limit_bytes=20 * MIB),
        cost_estimate=pl.CostEstimate(flops=flops, bytes_accessed=8 * MIB, transcendentals=0),
    )
    query_call = pl.pallas_call(
        functools.partial(query_kernel, local_levels, bit_count, head_count),
        in_specs=[vmem] * 7,
        out_specs=[vmem] * 2,
        out_shape=[
            jax.ShapeDtypeStruct(queries.shape, jnp.bfloat16),
            jax.ShapeDtypeStruct(level_coef.shape, jnp.float32),
        ],
        scratch_shapes=[pltpu.VMEM((head_count, key_width, tokens), jnp.bfloat16)],
        compiler_params=pltpu.CompilerParams(vmem_limit_bytes=12 * MIB),
        cost_estimate=pl.CostEstimate(flops=flops // 4, bytes_accessed=6 * MIB, transcendentals=0),
    )
    query_in, key_in, value_in, grad_in, gates_in, states_in = inputs
    key_local, value_local, coef_grad, grad_weights, *contrib = local_call(
        query_in, key_in, value_in, grad_in, gates_in, grad_t
    )
    query_grad, coef_grad = query_call(query_in, key_in, grad_in, gates_in, states_in, grad_weights, coef_grad)

    grad_state = [jnp.zeros(shape.shape, jnp.float32) for shape in state_shapes]
    for level_idx in reversed(range(bit_count - 1)):
        for part in parts:
            grad_state[part] = grad_state[part] + received[part]
            own = contrib[level_idx * len(chunks) + part]
            received[part] = exchange(grad_state[part] + own, "seq", level_idx)

    head_bits = lax.axis_size("head").bit_length() - 1
    coef_received = jnp.zeros_like(coef_grad)
    for bit_pos in reversed(range(head_bits)):
        if bit_pos < head_bits - 1:
            coef_grad = coef_grad + coef_received
        coef_received = exchange(coef_grad, "head", bit_pos)

    shapes = [
        jax.ShapeDtypeStruct(queries.shape, jnp.bfloat16),
        jax.ShapeDtypeStruct(values.shape, jnp.bfloat16),
    ]
    coef_shape = jax.ShapeDtypeStruct(level_coef.shape, jnp.float32)
    early = [head for head in range(head_count) if (head + 1) * value_width <= chunks[0][1]]
    late = [head for head in range(head_count) if head not in early]
    common = (inputs[1], inputs[2], key_local, value_local)

    def apply_call(which, chunk_count, last):
        pieces = 2 * len(which) * (tokens // wide) + 1
        in_count = 4 + 2 * chunk_count + 1 + last
        return pl.pallas_call(
            functools.partial(apply_kernel, head_count, which, chunk_count, last),
            in_specs=[vmem] * in_count + [hbm] * (2 * last),
            out_specs=[hbm] * 3,
            out_shape=shapes + [coef_shape] if last else shapes[:1] + shapes,
            input_output_aliases={in_count: 0, in_count + 1: 1} if last else {},
            scratch_shapes=[
                pltpu.VMEM((len(which), tokens, key_width), jnp.bfloat16),
                pltpu.VMEM((len(which), tokens, value_width), jnp.bfloat16),
            ]
            + [pltpu.VMEM(level_coef.shape, jnp.float32)] * last
            + [pltpu.SemaphoreType.DMA((pieces,))],
            compiler_params=pltpu.CompilerParams(vmem_limit_bytes=12 * MIB),
        )

    query_grad, *outs = apply_call(early, 1, False)(*common, grad_state[0], received[0], query_grad)
    outs = [pltpu.with_memory_space_constraint(x, pltpu.HBM) for x in outs]
    key_grad, value_grad, coef_grad = apply_call(late, 2, True)(
        *common, *grad_state, *received, coef_grad, coef_received, *outs
    )
    return (query_grad, key_grad, value_grad, coef_grad)


def solution(mesh):
    in_specs = (
        P("seq", "head"),
        P("seq", "head"),
        P("seq", "head"),
        P("seq", "head"),
        P(None, "seq"),
        P("seq", None, "head", None, None),
    )
    out_specs = (P("seq", "head"), P("seq", "head"), P("seq", "head"), P(None, "seq"))

    return jax.shard_map(shards, mesh=mesh, in_specs=in_specs, out_specs=out_specs, check_vma=False)
```

```python
import functools

import jax
import jax.numpy as jnp
from jax import lax
from jax.experimental import pallas as pl
from jax.experimental.pallas import tpu as pltpu
from jax.sharding import PartitionSpec as P


LANES = 128
TOP_PIECES = 2
SUBLANES = 8
MIB = 2**20


def level_weight(level_idx):
    if level_idx == 0:
        return 1.0
    return 2.0 ** (-(level_idx - 1) / 2.0)


def dot(lhs, rhs):
    return jnp.dot(lhs, rhs, preferred_element_type=jnp.float32)


def dot_t(lhs, rhs):
    return lax.dot_general(lhs, rhs, (((1,), (1,)), ((), ())), preferred_element_type=jnp.float32)


def chunk_rows(head_count, value_width):
    rows = head_count * value_width
    cut = rows // 2 // 16 * 16
    return ((0, cut), (cut, rows))


def store_rows(refs, chunks, head, state):
    width = state.shape[0]
    for ref, (start, stop) in zip(refs, chunks):
        low, high = max(start, head * width), min(stop, (head + 1) * width)
        if low < high:
            ref[low - start : high - start, :] = state[low - head * width : high - head * width]


def load_rows(refs, chunks, head, width):
    parts = []
    for ref, (start, stop) in zip(refs, chunks):
        low, high = max(start, head * width), min(stop, (head + 1) * width)
        if low < high:
            parts.append(ref[low - start : high - start, :])
    return parts[0] if len(parts) == 1 else jnp.concatenate(parts, axis=0)


def shard_bit(level_idx):
    return jnp.bitwise_and(jnp.right_shift(lax.axis_index("seq"), level_idx), 1).astype(jnp.float32)


def state_gradients(rows, query, grad_t, gates_ref):
    grad_t = grad_t.astype(jnp.float32)
    scaled = [(gates_ref[row : row + 1, :] * grad_t).astype(jnp.bfloat16) for row in rows]
    return dot(jnp.concatenate(scaled, axis=0), query)


def top_kernel(head_count, level_idx, row, *refs):
    query_hbm, key_hbm, value_hbm, grad_hbm, gates_hbm, states_hbm = refs[:6]
    query, key, value, grad, gates, states, grad_t, *out_refs, sems = refs[6:]
    key_width = query.shape[1] // head_count
    value_width = grad.shape[1] // head_count
    chunks = chunk_rows(head_count, value_width)
    size = query.shape[0] // TOP_PIECES
    spans = [slice(part * size, (part + 1) * size) for part in range(TOP_PIECES)]
    levels = slice(0, level_idx + 1)
    pairs = [(gates_hbm, gates)]
    for span in spans:
        pairs += [(grad_hbm.at[span, :], grad.at[span, :]), (query_hbm.at[span, :], query.at[span, :])]
    pairs += [(key_hbm, key), (value_hbm, value), (states_hbm.at[:, levels], states.at[:, levels])]
    copies = [pltpu.make_async_copy(source, target, sems.at[k]) for k, (source, target) in enumerate(pairs)]
    for copy in copies:
        copy.start()
    copies[0].wait()
    totals = [0.0] * head_count
    for part, span in enumerate(spans):
        copies[1 + 2 * part].wait()
        copies[2 + 2 * part].wait()
        for head in range(head_count):
            keys = slice(head * key_width, (head + 1) * key_width)
            flipped = grad[span, head * value_width : (head + 1) * value_width].T
            grad_t[head, :, span] = flipped
            totals[head] += state_gradients([row], query[span, keys], flipped, gates.at[:, span])
    scale = shard_bit(level_idx) * level_weight(row)
    for head, total in enumerate(totals):
        store_rows(out_refs, chunks, head, total * scale)
    for copy in copies[1 + 2 * len(spans) :]:
        copy.wait()


def within_block(block):
    col = lax.broadcasted_iota(jnp.int32, (SUBLANES, block), 0)
    row = jnp.bitwise_and(lax.broadcasted_iota(jnp.int32, (SUBLANES, block), 1), SUBLANES - 1)
    mixed = jnp.bitwise_xor(row, col)
    level = jnp.zeros((SUBLANES, block), jnp.int32)
    for bit_pos in range(SUBLANES.bit_length() - 1):
        level = level + (jnp.right_shift(mixed, bit_pos) > 0).astype(jnp.int32)
    return jnp.where(col <= row, level, -1)


def local_kernel(
    local_levels, cross_levels, head_count,
    query_ref, key_ref, value_ref, grad_ref, gates_ref, grad_t,
    key_out, value_out, coef_out, grad_weights_out, *rest,
):
    *state_outs, mix, sums, weights = rest
    tokens = query_ref.shape[0]
    key_width = query_ref.shape[1] // head_count
    value_width = value_ref.shape[1] // head_count
    block = LANES
    wide = 2 * block
    base = block.bit_length() - 1
    inner = SUBLANES.bit_length() - 1
    groups = block // SUBLANES

    level_in = within_block(block)
    lane_group = jnp.right_shift(lax.broadcasted_iota(jnp.int32, (SUBLANES, block), 1), inner)
    row_group = jnp.right_shift(lax.broadcasted_iota(jnp.int32, (groups, block), 1), inner)
    col_group = lax.broadcasted_iota(jnp.int32, (groups, block), 0)
    mixed = jnp.bitwise_xor(row_group, col_group)
    level_out = jnp.zeros((groups, block), jnp.int32)
    for bit_pos in range(base - inner):
        level_out = level_out + (jnp.right_shift(mixed, bit_pos) > 0).astype(jnp.int32)
    level_out = jnp.where(col_group < row_group, level_out + inner, -1)

    for idx in range(tokens // block):
        gates = [
            gates_ref[level : level + 1, idx * block : (idx + 1) * block] * level_weight(level)
            for level in range(base + 1)
        ]
        inside = jnp.zeros((SUBLANES, block), jnp.float32)
        for level in range(inner + 1):
            inside = jnp.where(level_in == level, gates[level], inside)
        outside = jnp.zeros((groups, block), jnp.float32)
        for level in range(inner + 1, base + 1):
            outside = jnp.where(level_out == level, gates[level], outside)
        for group in range(groups):
            mix[idx, group * SUBLANES : (group + 1) * SUBLANES, :] = jnp.where(
                lane_group == group, inside, outside[group : group + 1, :]
            )

    def diagonal_sums(product):
        parts = [product[group * SUBLANES : (group + 1) * SUBLANES, :] for group in range(groups)]
        inside = parts[0]
        for group in range(1, groups):
            inside = jnp.where(lane_group == group, parts[group], inside)
        totals = [jnp.where(level_in == level, inside, 0.0) for level in range(inner + 1)]
        for level in range(inner + 1, base + 1):
            picked = parts[0]
            for pair in range(1, len(parts) // 2):
                picked = jnp.where(jnp.right_shift(lane_group, level - inner) == pair, parts[2 * pair], picked)
            right = jnp.bitwise_and(jnp.right_shift(lane_group, level - inner - 1), 1) == 1
            totals.append(jnp.where(right, picked, 0.0))
            parts = [parts[2 * pair] + parts[2 * pair + 1] for pair in range(len(parts) // 2)]
        return [jnp.sum(total, axis=0, keepdims=True) for total in totals]

    for t_start in range(0, tokens, wide):
        t_end = t_start + wide
        t_slice = slice(t_start, t_end)
        idx = t_start // block
        low = slice(t_start, t_start + block)
        high = slice(t_start + block, t_end)
        near = base + 1
        chunks = []
        s_start = 0
        while s_start < t_start:
            level = (s_start ^ t_start).bit_length()
            size = min(1 << (level - 1), t_start - s_start)
            chunks.append((s_start, s_start + size, level))
            s_start += size
        level_sums = {}
        for head in range(head_count):
            keys = slice(head * key_width, (head + 1) * key_width)
            vals = slice(head * value_width, (head + 1) * value_width)
            q_rows = query_ref[t_slice, keys]
            g_rows = grad_ref[t_slice, vals]
            grad_weights = grad_weights_out.at[head, t_start // wide]
            for s_start, s_end, level in chunks:
                s_slice = slice(s_start, s_end)
                gate = gates_ref[level : level + 1, t_slice] * level_weight(level)
                score = dot_t(key_ref[s_slice, keys], q_rows)
                grad_score = dot_t(value_ref[s_slice, vals], g_rows)
                product = jnp.sum((score * grad_score).reshape(-1, SUBLANES, wide), axis=0)
                level_sums[level] = level_sums[level] + product if level in level_sums else product
                weights[s_slice, :] = (gate * score).astype(jnp.bfloat16)
                grad_weights[s_slice, :] = (gate * grad_score).astype(jnp.bfloat16)
            score = dot_t(key_ref[t_slice, keys], q_rows)
            grad_score = dot_t(value_ref[t_slice, vals], g_rows)
            product = score * grad_score
            gate = jnp.broadcast_to(gates_ref[near : near + 1, high] * level_weight(near), (block, block))
            tile = jnp.concatenate([mix[idx], gate], axis=1)
            weights[low, :] = (tile * score[:block]).astype(jnp.bfloat16)
            grad_weights[low, :] = (tile * grad_score[:block]).astype(jnp.bfloat16)
            zeros = jnp.zeros((block, block), jnp.bfloat16)
            tile = mix[idx + 1]
            weights[high, :block] = zeros
            grad_weights[high, :block] = zeros
            weights[high, block:] = (tile * score[block:, block:]).astype(jnp.bfloat16)
            grad_weights[high, block:] = (tile * grad_score[block:, block:]).astype(jnp.bfloat16)
            three = [product[:block, :block], product[:block, block:], product[block:, block:]]
            if head > 0:
                three = [part + sums[k] for k, part in enumerate(three)]
            if head < head_count - 1:
                for k, part in enumerate(three):
                    sums[k] = part

            s_all = slice(0, t_end)
            key_part = dot(grad_weights[s_all, :], q_rows)
            value_part = dot(weights[s_all, :], g_rows)
            key_out[t_slice, keys] = key_part[t_start:]
            value_out[t_slice, vals] = value_part[t_start:]
            if t_start:
                key_out[:t_start, keys] += key_part[:t_start]
                value_out[:t_start, vals] += value_part[:t_start]

        for level in range(near + 1, local_levels):
            if level in level_sums:
                total = jnp.sum(level_sums[level], axis=0, keepdims=True) * level_weight(level)
            else:
                total = jnp.zeros((1, wide), jnp.float32)
            coef_out[level : level + 1, t_slice] = total
        coef_out[near : near + 1, low] = jnp.zeros((1, block), jnp.float32)
        coef_out[near : near + 1, high] = jnp.sum(three[1], axis=0, keepdims=True) * level_weight(near)
        for part, where in ((three[0], low), (three[2], high)):
            for level, total in enumerate(diagonal_sums(part)):
                coef_out[level : level + 1, where] = total * level_weight(level)
    rows = [local_levels + level_idx for level_idx in range(cross_levels - 1)]
    chunks = chunk_rows(head_count, value_width)
    for head in range(head_count):
        if not rows:
            break
        keys = slice(head * key_width, (head + 1) * key_width)
        stacked = state_gradients(rows, query_ref[:, keys], grad_t[head], gates_ref)
        for level_idx, row in enumerate(rows):
            part = stacked[level_idx * value_width : (level_idx + 1) * value_width]
            refs = state_outs[level_idx * len(chunks) : (level_idx + 1) * len(chunks)]
            store_rows(refs, chunks, head, part * (shard_bit(level_idx) * level_weight(row)))


def query_kernel(
    local_levels, cross_levels, head_count,
    query_ref, key_ref, grad_ref, gates_ref, states_ref, grad_weights_ref, coef_ref, query_out, coef_out, key_t,
):
    tokens = query_ref.shape[0]
    key_width = query_ref.shape[1] // head_count
    value_width = grad_ref.shape[1] // head_count
    wide = grad_weights_ref.shape[3]
    coef_out[:local_levels, :] = coef_ref[:local_levels, :]
    for t_start in range(0, tokens, wide):
        t_end = t_start + wide
        t_slice = slice(t_start, t_end)
        cross_sums = [None] * cross_levels
        for head in range(head_count):
            keys = slice(head * key_width, (head + 1) * key_width)
            vals = slice(head * value_width, (head + 1) * value_width)
            key_t[head, :, t_slice] = key_ref[t_slice, keys].T
            total = dot(key_t[head, :, :t_end], grad_weights_ref[head, t_start // wide, :t_end, :])
            stacked = states_ref[0, :cross_levels, head].reshape(cross_levels * key_width, value_width)
            projected = dot_t(stacked, grad_ref[t_slice, vals])
            q_wide = query_ref[t_slice, keys].T.astype(jnp.float32)
            for level_idx in range(cross_levels):
                row = local_levels + level_idx
                part = projected[level_idx * key_width : (level_idx + 1) * key_width]
                total += (gates_ref[row : row + 1, t_slice] * shard_bit(level_idx)) * part
                cross = jnp.sum((q_wide * part).reshape(-1, SUBLANES, wide), axis=0)
                cross_sums[level_idx] = cross if head == 0 else cross_sums[level_idx] + cross
            query_out[t_slice, keys] = total.astype(jnp.bfloat16).T
        for level_idx, cross in enumerate(cross_sums):
            row = local_levels + level_idx
            coef_out[row : row + 1, t_slice] = jnp.sum(cross, axis=0, keepdims=True) * shard_bit(level_idx)


def apply_kernel(head_count, heads, chunk_count, last, *refs):
    key_ref, value_ref, key_local, value_local = refs[:4]
    state_refs = refs[4 : 4 + chunk_count]
    received_refs = refs[4 + chunk_count : 4 + 2 * chunk_count]
    tokens = key_ref.shape[0]
    key_width = key_ref.shape[1] // head_count
    value_width = value_ref.shape[1] // head_count
    chunks = chunk_rows(head_count, value_width)[:chunk_count]
    wide = 2 * LANES
    copies = []
    if last:
        coef_ref, coef_received = refs[-11:-9]
        key_out, value_out, coef_out, key_total, value_total, coef_total, sems = refs[-7:]
        used = coef_ref.shape[0]
        coef_total[:used, :] = coef_ref[...] + coef_received[...]
        if used < coef_total.shape[0]:
            coef_total[used:, :] = jnp.zeros((coef_total.shape[0] - used, tokens), jnp.float32)
        copies.append(pltpu.make_async_copy(coef_total, coef_out, sems.at[0]))
        copies[0].start()
    else:
        query_ref = refs[4 + 2 * chunk_count]
        query_out, key_out, value_out, key_total, value_total, sems = refs[-6:]
        copies.append(pltpu.make_async_copy(query_ref, query_out, sems.at[0]))
        copies[0].start()
    for place, head in enumerate(heads):
        keys = slice(head * key_width, (head + 1) * key_width)
        vals = slice(head * value_width, (head + 1) * value_width)
        state = load_rows(state_refs, chunks, head, value_width) + load_rows(received_refs, chunks, head, value_width)
        state = state.astype(jnp.bfloat16)
        for start in range(0, tokens, wide):
            part = slice(start, start + wide)
            key_total[place, part, :] = (key_local[part, keys] + dot(value_ref[part, vals], state)).astype(jnp.bfloat16)
            value_total[place, part, :] = (value_local[part, vals] + dot_t(key_ref[part, keys], state)).astype(
                jnp.bfloat16
            )
            for source, target, cols in ((key_total, key_out, keys), (value_total, value_out, vals)):
                copy = pltpu.make_async_copy(source.at[place, part, :], target.at[part, cols], sems.at[len(copies)])
                copy.start()
                copies.append(copy)
    for copy in copies:
        copy.wait()


def shards(queries, key_vectors, values, out_grad, level_coef, saved_states):
    tokens, _ = queries.shape
    cross_levels = saved_states.shape[1]
    head_count = saved_states.shape[2]
    key_width = saved_states.shape[3]
    value_width = saved_states.shape[4]
    local_levels = level_coef.shape[0] - cross_levels
    shard_count = lax.axis_size("seq")
    bit_count = shard_count.bit_length() - 1
    block = LANES
    wide = 2 * block
    vmem = pl.BlockSpec(memory_space=pltpu.VMEM)
    hbm = pl.BlockSpec(memory_space=pltpu.HBM)
    chunks = chunk_rows(head_count, value_width)
    parts = range(len(chunks))
    state_shapes = [jax.ShapeDtypeStruct((stop - start, key_width), jnp.float32) for start, stop in chunks]

    inputs = (queries, key_vectors, values, out_grad, level_coef, saved_states)
    count = len(inputs)
    results = pl.pallas_call(
        functools.partial(top_kernel, head_count, bit_count - 1, local_levels + bit_count - 1),
        in_specs=[hbm] * 6,
        out_specs=[vmem] * (count + 1 + len(chunks)),
        out_shape=[jax.ShapeDtypeStruct(x.shape, x.dtype) for x in inputs]
        + [jax.ShapeDtypeStruct((head_count, value_width, tokens), jnp.bfloat16)]
        + state_shapes,
        scratch_shapes=[pltpu.SemaphoreType.DMA((2 * TOP_PIECES + 4,))],
        compiler_params=pltpu.CompilerParams(vmem_limit_bytes=8 * MIB),
    )(*[pltpu.with_memory_space_constraint(x, pltpu.HBM) for x in inputs])
    inputs, grad_t, tops = results[:count], results[count], results[count + 1 :]

    def exchange(value, axis, bit_pos):
        pairs = [(p, p ^ 2**bit_pos) for p in range(lax.axis_size(axis))]
        return lax.ppermute(value, axis, pairs)

    received = [exchange(tops[part], "seq", bit_count - 1) for part in parts]

    flops = 8 * head_count * tokens * tokens * key_width
    blocks = tokens // wide
    local_call = pl.pallas_call(
        functools.partial(local_kernel, local_levels, bit_count, head_count),
        in_specs=[vmem] * 6,
        out_specs=[vmem] * (4 + (bit_count - 1) * len(chunks)),
        out_shape=[
            jax.ShapeDtypeStruct(queries.shape, jnp.float32),
            jax.ShapeDtypeStruct(values.shape, jnp.float32),
            jax.ShapeDtypeStruct(level_coef.shape, jnp.float32),
            jax.ShapeDtypeStruct((head_count, blocks, tokens, wide), jnp.bfloat16),
        ]
        + state_shapes * (bit_count - 1),
        scratch_shapes=[
            pltpu.VMEM((tokens // block, block, block), jnp.float32),
            pltpu.VMEM((3, block, block), jnp.float32),
            pltpu.VMEM((tokens, wide), jnp.bfloat16),
        ],
        compiler_params=pltpu.CompilerParams(vmem_limit_bytes=20 * MIB),
        cost_estimate=pl.CostEstimate(flops=flops, bytes_accessed=8 * MIB, transcendentals=0),
    )
    query_call = pl.pallas_call(
        functools.partial(query_kernel, local_levels, bit_count, head_count),
        in_specs=[vmem] * 7,
        out_specs=[vmem] * 2,
        out_shape=[
            jax.ShapeDtypeStruct(queries.shape, jnp.bfloat16),
            jax.ShapeDtypeStruct((local_levels + bit_count, tokens), jnp.float32),
        ],
        scratch_shapes=[pltpu.VMEM((head_count, key_width, tokens), jnp.bfloat16)],
        compiler_params=pltpu.CompilerParams(vmem_limit_bytes=12 * MIB),
        cost_estimate=pl.CostEstimate(flops=flops // 4, bytes_accessed=6 * MIB, transcendentals=0),
    )
    query_in, key_in, value_in, grad_in, gates_in, states_in = inputs
    key_local, value_local, coef_grad, grad_weights, *contrib = local_call(
        query_in, key_in, value_in, grad_in, gates_in, grad_t
    )
    query_grad, coef_grad = query_call(query_in, key_in, grad_in, gates_in, states_in, grad_weights, coef_grad)

    grad_state = [jnp.zeros(shape.shape, jnp.float32) for shape in state_shapes]
    for level_idx in reversed(range(bit_count - 1)):
        for part in parts:
            grad_state[part] = grad_state[part] + received[part]
            own = contrib[level_idx * len(chunks) + part]
            received[part] = exchange(grad_state[part] + own, "seq", level_idx)

    head_bits = lax.axis_size("head").bit_length() - 1
    coef_received = jnp.zeros_like(coef_grad)
    for bit_pos in reversed(range(head_bits)):
        if bit_pos < head_bits - 1:
            coef_grad = coef_grad + coef_received
        coef_received = exchange(coef_grad, "head", bit_pos)

    shapes = [
        jax.ShapeDtypeStruct(queries.shape, jnp.bfloat16),
        jax.ShapeDtypeStruct(values.shape, jnp.bfloat16),
    ]
    coef_shape = jax.ShapeDtypeStruct(level_coef.shape, jnp.float32)
    early = [head for head in range(head_count) if (head + 1) * value_width <= chunks[0][1]]
    late = [head for head in range(head_count) if head not in early]
    common = (inputs[1], inputs[2], key_local, value_local)

    def apply_call(which, chunk_count, last):
        pieces = 2 * len(which) * (tokens // wide) + 1
        in_count = 4 + 2 * chunk_count + 1 + last
        return pl.pallas_call(
            functools.partial(apply_kernel, head_count, which, chunk_count, last),
            in_specs=[vmem] * in_count + [hbm] * (2 * last),
            out_specs=[hbm] * 3,
            out_shape=shapes + [coef_shape] if last else shapes[:1] + shapes,
            input_output_aliases={in_count: 0, in_count + 1: 1} if last else {},
            scratch_shapes=[
                pltpu.VMEM((len(which), tokens, key_width), jnp.bfloat16),
                pltpu.VMEM((len(which), tokens, value_width), jnp.bfloat16),
            ]
            + [pltpu.VMEM(level_coef.shape, jnp.float32)] * last
            + [pltpu.SemaphoreType.DMA((pieces,))],
            compiler_params=pltpu.CompilerParams(vmem_limit_bytes=12 * MIB),
        )

    query_grad, *outs = apply_call(early, 1, False)(*common, grad_state[0], received[0], query_grad)
    outs = [pltpu.with_memory_space_constraint(x, pltpu.HBM) for x in outs]
    key_grad, value_grad, coef_grad = apply_call(late, 2, True)(
        *common, *grad_state, *received, coef_grad, coef_received, *outs
    )
    return (query_grad, key_grad, value_grad, coef_grad)


def solution(mesh):
    in_specs = (
        P("seq", "head"),
        P("seq", "head"),
        P("seq", "head"),
        P("seq", "head"),
        P(None, "seq"),
        P("seq", None, "head", None, None),
    )
    out_specs = (P("seq", "head"), P("seq", "head"), P("seq", "head"), P(None, "seq"))

    return jax.shard_map(shards, mesh=mesh, in_specs=in_specs, out_specs=out_specs, check_vma=False)
```
